512 devices in a mesh: narrow: 16 (over x, y_lo, core), wide: 32 (over y_hi, z).
Axes of the slice: x: 4, y: 4 (y_hi: 2, y_lo: 2; y = y_hi * 2 + y_lo), z: 16, core: 2. Of those that a mesh axis runs over, the one named last changes fastest.
Arguments:
- vectors: float32 [512, 24576], P('wide', 'narrow'), may hold values from -63 to 63
- blocks: float32 [192, 5, 128, 128], P('narrow'), may hold values from -0.125 to 0.125
- columns: int32 [192, 5], P('narrow'), may hold values from 0 to 191, as said below
- lower_bound: float32 [1], replicated, may hold values from -0.8 to -0.2
- upper_bound: float32 [1], replicated, may hold values from 2.2 to 2.8
Outputs:
- basis: float32 [512, 24576], P(None, ('narrow', 'wide'))
The draws below stay inside these ranges and needn't reach their ends.
Inputs may be any that keep to these rules, and one draw needn't show every extreme that they name: `columns`: row r holds 5 different block-rows, each within 3 of r along the closed loop of 192 block-rows (indices taken modulo 192); r - 1 and r + 1 appear in every row, r - 3 in every even row and r + 3 in every odd row.
All inputs are finite; a program needn't handle non-finite values.
Results may differ from the reference program's by a relative error of at most 0.0001.
Values sent between devices are 32-bit elements; how exact they have to be, the bound alone decides.
A program may use at most 64 MiB of HBM per device.

```python
import jax
import jax.numpy as jnp
from jax import lax

K = 512
BLOCK = 128
SLOTS = 5
REACH = 3
STEPS = 8
NB = 192
N = 24576


def draw_vectors(key, part):
    key_main = jax.random.fold_in(key, 11)
    key_cols = jax.random.fold_in(key, 12)
    noise = jnp.clip(jax.random.normal(key_main, (K, N), jnp.float32), -5.0, 5.0)
    col_scale = jnp.exp(jax.random.uniform(key_cols, (K, 1), jnp.float32, jnp.log(0.3), jnp.log(3.0)))
    row_scale = jnp.exp(jnp.log(3.0) * jnp.arange(N, dtype=jnp.float32) / N)[None, :]
    return noise * col_scale * row_scale


def draw_columns(key, part):
    key_pick = jax.random.fold_in(key, 21)
    block_ids = jnp.arange(NB, dtype=jnp.int32)
    far_side = jnp.where(block_ids % 2 == 0, -REACH, REACH).astype(jnp.int32)
    middle = jnp.array([-(REACH - 1), 0, REACH - 1], dtype=jnp.int32)
    candidates = jnp.concatenate([jnp.broadcast_to(middle[None, :], (NB, 3)), (-far_side)[:, None]], axis=1)
    scores = jax.random.randint(key_pick, (NB, 4), 0, 1 << 20) * 4 + jnp.arange(4, dtype=jnp.int32)[None, :]
    order = jnp.argsort(scores, axis=1)[:, :2]
    chosen = jnp.take_along_axis(candidates, order, axis=1)
    offsets = jnp.concatenate([jnp.full((NB, 1), -1, jnp.int32), jnp.full((NB, 1), 1, jnp.int32), far_side[:, None], chosen], axis=1)
    return ((block_ids[:, None] + offsets) % NB).astype(jnp.int32)


def block_scale(key, extent, split, smallest, high):
    def one(axis_at, parts):
        draws = jax.random.uniform(jax.random.fold_in(jax.random.fold_in(key, 6), axis_at), (parts,), jnp.float32, smallest / len(split), high / len(split))
        return jnp.repeat(jnp.exp(draws), extent[axis_at] // parts).reshape((-1,) + (1,) * (len(extent) - axis_at - 1))

    level = one(*split[0])
    for cut in split[1:]:
        level = level * one(*cut)
    return level


def normal_values(key, dims, scale, bound, split=(), held_as=jnp.bfloat16):
    gain = block_scale(key, dims, split, -0.22, 0.18) if split else 1.0
    values = jax.random.normal(key, dims, jnp.float32) * scale * gain
    return jnp.minimum(jnp.maximum(values, -bound), bound).astype(held_as)


def setup_inputs(seed: int = 0) -> dict:
    keys = jax.random.split(jax.random.key(seed), 6)
    vectors = draw_vectors(jax.random.fold_in(keys[5], 71), 0)
    blocks = normal_values(keys[1], (NB, SLOTS, BLOCK, BLOCK), (20 * BLOCK) ** -0.5, 0.125, ((0, 16),), jnp.float32)
    columns = draw_columns(jax.random.fold_in(keys[5], 71), 0)
    lower_bound = jnp.clip(jax.random.uniform(keys[3], (1,), jnp.float32, -0.8, -0.2), -0.8, -0.2)
    upper_bound = jnp.clip(jax.random.uniform(keys[4], (1,), jnp.float32, 2.2, 2.8), 2.2, 2.8)
    return {"vectors": vectors, "blocks": blocks, "columns": columns, "lower_bound": lower_bound, "upper_bound": upper_bound}


def operate(source, blocks, columns):
    count = source.shape[0]
    nblocks = blocks.shape[0]
    bsize = blocks.shape[2]
    tile_rows = source.reshape(count, nblocks, bsize)
    summed = jnp.zeros_like(tile_rows)
    for slot in range(blocks.shape[1]):
        picked = tile_rows[:, columns[:, slot], :]
        summed = summed + jnp.einsum('rij,krj->kri', blocks[:, slot], picked, precision=lax.Precision.HIGHEST)
    return source + summed.reshape(count, nblocks * bsize)

def reference(vectors, blocks, columns, lower_bound, upper_bound):
    centre = (upper_bound[0] + lower_bound[0]) * 0.5
    half_width = (upper_bound[0] - lower_bound[0]) * 0.5
    previous = vectors
    current = (operate(vectors, blocks, columns) - centre * vectors) / half_width
    for step in range(STEPS - 1):
        following = 2.0 * (operate(current, blocks, columns) - centre * current) / half_width - previous
        previous = current
        current = following
    gram_matrix = jnp.dot(current, current.T, preferred_element_type=jnp.float32, precision=lax.Precision.HIGHEST)
    frob_norm = jnp.sqrt(jnp.sum(gram_matrix * gram_matrix) + 1e-06)
    rotation = 1.5 * jnp.eye(K, dtype=gram_matrix.dtype) - 0.5 * gram_matrix / frob_norm
    rotated = jnp.dot(rotation, current, preferred_element_type=jnp.float32, precision=lax.Precision.HIGHEST)
    return jnp.sqrt(N / frob_norm) * rotated
```

```python
import functools
import math

import jax
import jax.numpy as jnp
from jax import lax
from jax.experimental import pallas as pl
from jax.experimental.pallas import tpu as pltpu
from jax.sharding import PartitionSpec as P

REACH = 3
STEPS = 8
LANES = 128
SUB = 8
HALVES = 2
Z_SIZE = 16
MESH = pl.DeviceIdType.MESH
F32 = jnp.float32
BF16 = jnp.bfloat16


def split_pair(value):
    high = value.astype(BF16).astype(F32)
    return high, value - high


def upper_blocks(count):
    return [(i, j) for i in range(count) for j in range(i, count)]


def kernel_body(
    cfg,
    cols_ref,
    low_ref,
    up_ref,
    vec_ref,
    blk_ref,
    out_ref,
    ybuf,
    wbuf,
    stage,
    local_cols,
    pack,
    arrived,
    fmat,
    amat,
    bmat,
    gram,
    plane_in,
    plane_sum,
    z_in,
    z_sum,
    full,
    ghi,
    glo,
    halo_send,
    halo_recv,
    send_sem,
    a2a_recv,
    plane_recv,
    z_recv,
    bcast_recv,
    gather_recv,
):
    narrow, wide, z_size = cfg
    rows_here, slots = cols_ref.shape
    vecs = vec_ref.shape[0]
    total = rows_here * narrow
    planes = wide // z_size
    plane = narrow * planes
    n = lax.axis_index("narrow")
    w = lax.axis_index("wide")
    z = w % z_size
    y = w // z_size
    q = y * narrow + n
    right, left = lax.rem(n + 1, narrow), lax.rem(n + narrow - 1, narrow)
    share = rows_here * LANES // wide

    def plane_device(index):
        return (index % narrow, (index // narrow) * z_size + z)

    barrier = pltpu.get_barrier_semaphore()

    def greet_wide(k, carry):
        pl.semaphore_signal(barrier, inc=1, device_id=(n, (w + k) % wide), device_id_type=MESH)
        return carry

    def greet_plane(k, carry):
        pl.semaphore_signal(barrier, inc=1, device_id=plane_device((q + k) % plane), device_id_type=MESH)
        return carry

    lax.fori_loop(1, wide, greet_wide, 0)
    lax.fori_loop(1, plane, greet_plane, 0)

    first = n * rows_here
    for r in range(rows_here):
        for s in range(slots):
            at = cols_ref[r, s] - first + REACH
            at = jnp.where(at < 0, at + total, at)
            at = jnp.where(at >= total, at - total, at)
            local_cols[r, s] = jnp.minimum(at, rows_here + 2 * REACH - 1)

    for b in range(rows_here):
        ybuf[0, REACH + b] = vec_ref[:, b * LANES : (b + 1) * LANES]

    def split_blocks(r, carry):
        for s in range(slots):
            high, low = split_pair(blk_ref[r, s])
            wbuf[r, 0:LANES, s * LANES : (s + 1) * LANES] = high.astype(BF16)
            wbuf[r, LANES : 2 * LANES, s * LANES : (s + 1) * LANES] = low.astype(BF16)
        return carry

    lax.fori_loop(0, rows_here, split_blocks, 0)

    pl.semaphore_wait(barrier, wide + plane - 2)

    def halo_copies(j):
        leftward = pltpu.make_async_remote_copy(
            src_ref=ybuf.at[j, pl.ds(REACH, REACH)],
            dst_ref=ybuf.at[j, pl.ds(rows_here + REACH, REACH)],
            send_sem=halo_send.at[j, 0],
            recv_sem=halo_recv.at[j, 0],
            device_id=(left, w),
            device_id_type=MESH,
        )
        rightward = pltpu.make_async_remote_copy(
            src_ref=ybuf.at[j, pl.ds(rows_here, REACH)],
            dst_ref=ybuf.at[j, pl.ds(0, REACH)],
            send_sem=halo_send.at[j, 1],
            recv_sem=halo_recv.at[j, 1],
            device_id=(right, w),
            device_id_type=MESH,
        )
        return leftward, rightward

    for copy in halo_copies(0):
        copy.start()

    centre = jnp.full((vecs, LANES), (up_ref[0] + low_ref[0]) * 0.5, F32)
    inverse = 1.0 / jnp.full((vecs, LANES), (up_ref[0] - low_ref[0]) * 0.5, F32)
    keep = 1.0 - centre

    def put_stage(j, b):
        high, low = split_pair(ybuf[j, b])
        stage[b, 0:vecs, :] = high.astype(BF16)
        stage[b, vecs : 2 * vecs, :] = low.astype(BF16)

    edge = [r for r in range(rows_here) if r < REACH or r >= rows_here - REACH]
    inner = [r for r in range(rows_here) if r not in edge]

    def step(j, carry):
        alpha = inverse * jnp.where(j == 0, 1.0, 2.0).astype(F32)
        beta = jnp.where(j == 0, 0.0, 1.0).astype(F32)
        before = jnp.maximum(j - 1, 0)

        def row(r):
            x = jnp.concatenate([stage[local_cols[r, s]] for s in range(slots)], axis=1)
            o = lax.dot_general(x, wbuf[r], (((1,), (1,)), ((), ())), preferred_element_type=F32)
            prod = (o[:vecs, LANES:] + o[vecs:, :LANES]) + o[vecs:, LANES:] + o[:vecs, :LANES]
            ybuf[j + 1, REACH + r] = (keep * ybuf[j, REACH + r] + prod) * alpha - beta * ybuf[before, REACH + r]

        for b in range(REACH, REACH + rows_here):
            put_stage(j, b)
        for copy in halo_copies(j):
            copy.wait()
        for b in range(REACH):
            put_stage(j, b)
            put_stage(j, REACH + rows_here + b)
        for r in edge:
            row(r)

        @pl.when(j < STEPS - 1)
        def _():
            for copy in halo_copies(j + 1):
                copy.start()

        for r in inner:
            row(r)
        return carry

    lax.fori_loop(0, STEPS, step, 0)

    lane = lax.broadcasted_iota(jnp.int32, (SUB, LANES), 1)
    period = math.lcm(LANES, share) // share
    span = math.lcm(LANES, share) // LANES

    def pack_group(g, carry):
        for p in range(period):
            b0, off = divmod(p * share, LANES)
            parts = []
            for h in range(HALVES):
                here = ybuf[STEPS, REACH + g * span + b0, h * SUB : (h + 1) * SUB, :]
                part = pltpu.roll(here, (h * share - off) % LANES, 1) if (h * share - off) % LANES else here
                if off + share > LANES:
                    after = ybuf[STEPS, REACH + g * span + b0 + 1, h * SUB : (h + 1) * SUB, :]
                    part2 = pltpu.roll(after, (h * share + LANES - off) % LANES, 1)
                    part = jnp.where(lane < h * share + LANES - off, part, part2)
                parts.append(part)
            pack[g * period + p] = jnp.where(lane < share, parts[0], parts[1])
        return carry

    lax.fori_loop(0, wide // period, pack_group, 0)

    def a2a_copy(peer, slot):
        return pltpu.make_async_remote_copy(
            src_ref=pack.at[peer],
            dst_ref=arrived.at[slot],
            send_sem=send_sem.at[peer],
            recv_sem=a2a_recv.at[slot],
            device_id=(n, peer),
            device_id_type=MESH,
        )

    def a2a_start(k, carry):
        a2a_copy((w + k) % wide, w).start()
        return carry

    def a2a_wait(k, carry):
        peer = (w + k) % wide
        a2a_copy(peer, peer).wait()
        return carry

    lax.fori_loop(1, wide, a2a_start, 0)
    arrived[w] = pack[w]
    lax.fori_loop(1, wide, a2a_wait, 0)

    lane2 = lax.broadcasted_iota(jnp.int32, (HALVES * SUB, LANES), 1)

    def unpack(v, carry):
        tile = arrived[v]
        x = jnp.concatenate([tile, pltpu.roll(tile, LANES - share, 1)], axis=0)
        x = jnp.where(lane2 < share, x, 0.0)
        high, low = split_pair(x)
        rows = pl.ds(pl.multiple_of(v * HALVES * SUB, HALVES * SUB), HALVES * SUB)
        fmat[rows, :] = x
        amat[rows, 0:LANES] = (high + pltpu.roll(low, share, 1)).astype(BF16)
        amat[rows, LANES : 2 * LANES] = high.astype(BF16)
        bmat[rows, 0:LANES] = (high + pltpu.roll(high, share, 1)).astype(BF16)
        bmat[rows, LANES : 2 * LANES] = low.astype(BF16)
        return carry

    lax.fori_loop(0, wide, unpack, 0)

    side = fmat.shape[0] // LANES
    blocks_of = upper_blocks(side)
    for index, (i, j) in enumerate(blocks_of):
        gram[index * LANES : (index + 1) * LANES, :] = lax.dot_general(
            amat[i * LANES : (i + 1) * LANES, :],
            bmat[j * LANES : (j + 1) * LANES, :],
            (((1,), (1,)), ((), ())),
            preferred_element_type=F32,
        )

    chunk = gram.shape[0] // plane

    def chunk_at(index):
        return pl.ds(pl.multiple_of(index * chunk, SUB), chunk)

    def plane_copy(peer, slot):
        return pltpu.make_async_remote_copy(
            src_ref=gram.at[chunk_at(peer)],
            dst_ref=plane_in.at[slot],
            send_sem=send_sem.at[peer],
            recv_sem=plane_recv.at[slot],
            device_id=plane_device(peer),
            device_id_type=MESH,
        )

    def plane_start(k, carry):
        plane_copy((q + k) % plane, q).start()
        return carry

    def plane_wait(k, acc):
        peer = (q + k) % plane
        plane_copy(peer, peer).wait()
        return acc + plane_in[peer]

    lax.fori_loop(1, plane, plane_start, 0)
    plane_sum[...] = lax.fori_loop(1, plane, plane_wait, gram[chunk_at(q), :])

    tiles = chunk // SUB
    stride = z_size // tiles
    away = (z - n + z_size * narrow) % z_size
    owner = (away % stride == 0) & (away < stride * tiles)
    mine = jnp.minimum(away // stride, tiles - 1)

    def owner_z(t):
        return (t * stride + n) % z_size

    def z_copy(t, slot):
        return pltpu.make_async_remote_copy(
            src_ref=plane_sum.at[pl.ds(t * SUB, SUB)],
            dst_ref=z_in.at[slot],
            send_sem=send_sem.at[t],
            recv_sem=z_recv.at[slot],
            device_id=(n, y * z_size + owner_z(t)),
            device_id_type=MESH,
        )

    def tile_at(t):
        return pl.ds(pl.multiple_of(q * chunk + t * SUB, SUB), SUB)

    def bcast_copy(peer_z, t):
        return pltpu.make_async_remote_copy(
            src_ref=z_sum,
            dst_ref=full.at[tile_at(t)],
            send_sem=send_sem.at[peer_z],
            recv_sem=bcast_recv.at[t],
            device_id=(n, y * z_size + peer_z),
            device_id_type=MESH,
        )

    for t in range(tiles):

        @pl.when(owner_z(t) != z)
        def _():
            z_copy(t, z).start()

    @pl.when(owner)
    def _():
        def take(k, acc):
            peer = (z + k) % z_size
            z_copy(mine, peer).wait_recv()
            return acc + z_in[peer]

        own = plane_sum[pl.ds(pl.multiple_of(mine * SUB, SUB), SUB), :]
        z_sum[...] = lax.fori_loop(1, z_size, take, own)

    for t in range(tiles):

        @pl.when(owner_z(t) != z)
        def _():
            z_copy(t, z).wait_send()

    @pl.when(owner)
    def _():
        def give(k, carry):
            bcast_copy((z + k) % z_size, mine).start()
            return carry

        def given(k, carry):
            bcast_copy((z + k) % z_size, mine).wait_send()
            return carry

        lax.fori_loop(1, z_size, give, 0)
        full[tile_at(mine), :] = z_sum[...]
        lax.fori_loop(1, z_size, given, 0)

    for t in range(tiles):

        @pl.when(owner_z(t) != z)
        def _():
            bcast_copy(z, t).wait_recv()

    def gather_copy(peer, slot):
        return pltpu.make_async_remote_copy(
            src_ref=full.at[chunk_at(slot)],
            dst_ref=full.at[chunk_at(slot)],
            send_sem=send_sem.at[peer],
            recv_sem=gather_recv.at[slot],
            device_id=plane_device(peer),
            device_id_type=MESH,
        )

    def gather_start(k, carry):
        gather_copy((q + k) % plane, q).start()
        return carry

    def gather_wait(k, carry):
        peer = (q + k) % plane
        gather_copy(peer, peer).wait()
        return carry

    lax.fori_loop(1, plane, gather_start, 0)
    lax.fori_loop(1, plane, gather_wait, 0)

    squares = jnp.zeros((SUB, LANES), F32)
    for index, (i, j) in enumerate(blocks_of):
        block = full[index * LANES : (index + 1) * LANES, :]
        power = jnp.sum((block * block).reshape(LANES // SUB, SUB, LANES), axis=0)
        squares = squares + (power if i == j else 2.0 * power)
        high, low = split_pair(block)
        ghi[i * LANES : (i + 1) * LANES, j * LANES : (j + 1) * LANES] = high.astype(BF16)
        glo[i * LANES : (i + 1) * LANES, j * LANES : (j + 1) * LANES] = low.astype(BF16)
        if i != j:
            ghi[j * LANES : (j + 1) * LANES, i * LANES : (i + 1) * LANES] = high.T.astype(BF16)
            glo[j * LANES : (j + 1) * LANES, i * LANES : (i + 1) * LANES] = low.T.astype(BF16)

    frob = jnp.sqrt(jnp.sum(squares, keepdims=True) + 1e-06)
    scale = jnp.sqrt((total * LANES) / frob)
    main = 1.5 * scale
    cross = 0.5 * scale / frob
    fpair = amat[:, 0:LANES]
    for i in range(side):
        rows = slice(i * LANES, (i + 1) * LANES)
        zhi = jnp.dot(ghi[rows, :], fpair, preferred_element_type=F32)
        zlo = jnp.dot(glo[rows, :], fpair, preferred_element_type=F32)
        prod = (pltpu.roll(zhi, LANES - share, 1) + zlo) + zhi
        res = main * fmat[rows, :] - cross * prod
        out_ref[rows, :] = res[:, :share]


def on_device(cfg, vectors, blocks, columns, lower_bound, upper_bound):
    narrow, wide, z_size = cfg
    vecs, width = vectors.shape
    rows_here, slots = columns.shape
    count = vecs * wide
    side = count // LANES
    plane = narrow * (wide // z_size)
    gram_rows = len(upper_blocks(side)) * LANES
    chunk = gram_rows // plane
    ext = rows_here + 2 * REACH
    smem = pl.BlockSpec(memory_space=pltpu.SMEM)
    vmem = pl.BlockSpec(memory_space=pltpu.VMEM)
    dma = pltpu.SemaphoreType.DMA
    return pl.pallas_call(
        functools.partial(kernel_body, cfg),
        out_shape=jax.ShapeDtypeStruct((count, width // wide), F32),
        in_specs=[smem, smem, smem, vmem, vmem],
        out_specs=vmem,
        scratch_shapes=[
            pltpu.VMEM((STEPS + 1, ext, vecs, LANES), F32),
            pltpu.VMEM((rows_here, 2 * LANES, slots * LANES), BF16),
            pltpu.VMEM((ext, 2 * vecs, LANES), BF16),
            pltpu.SMEM((rows_here, slots), jnp.int32),
            pltpu.VMEM((wide, SUB, LANES), F32),
            pltpu.VMEM((wide, SUB, LANES), F32),
            pltpu.VMEM((count, LANES), F32),
            pltpu.VMEM((count, 2 * LANES), BF16),
            pltpu.VMEM((count, 2 * LANES), BF16),
            pltpu.VMEM((gram_rows, LANES), F32),
            pltpu.VMEM((plane, chunk, LANES), F32),
            pltpu.VMEM((chunk, LANES), F32),
            pltpu.VMEM((z_size, SUB, LANES), F32),
            pltpu.VMEM((SUB, LANES), F32),
            pltpu.VMEM((gram_rows, LANES), F32),
            pltpu.VMEM((count, count), BF16),
            pltpu.VMEM((count, count), BF16),
            dma((STEPS, 2)),
            dma((STEPS, 2)),
            dma((max(wide, plane, z_size),)),
            dma((wide,)),
            dma((plane,)),
            dma((z_size,)),
            dma((chunk // SUB,)),
            dma((plane,)),
        ],
        compiler_params=pltpu.CompilerParams(
            collective_id=0, has_side_effects=True, vmem_limit_bytes=48 * 1024 * 1024
        ),
    )(columns, lower_bound, upper_bound, vectors, blocks)


def solution(mesh):
    cfg = (mesh.shape["narrow"], mesh.shape["wide"], Z_SIZE)
    return jax.shard_map(
        functools.partial(on_device, cfg),
        mesh=mesh,
        in_specs=(P("wide", "narrow"), P("narrow", None, None, None), P("narrow", None), P(), P()),
        out_specs=P(None, ("narrow", "wide")),
        check_vma=False,
    )
```

```python
import functools

import jax
import jax.numpy as jnp
from jax import lax
from jax.experimental import pallas as pl
from jax.experimental.pallas import tpu as pltpu
from jax.sharding import PartitionSpec as P

REACH = 3
STEPS = 8
LANES = 128
SUB = 8
HALVES = 2
Z_SIZE = 16
MESH = pl.DeviceIdType.MESH
F32 = jnp.float32
BF16 = jnp.bfloat16


def split_pair(value):
    high = value.astype(BF16).astype(F32)
    return high, value - high


def upper_blocks(count):
    return [(i, j) for i in range(count) for j in range(i, count)]


def kernel_body(
    cfg,
    cols_ref,
    low_ref,
    up_ref,
    vec_ref,
    blk_ref,
    out_ref,
    ybuf,
    wbuf,
    stage,
    local_cols,
    cols_in,
    blocks_in,
    pack,
    arrived,
    fmat,
    amat,
    bmat,
    gram,
    plane_in,
    plane_sum,
    z_in,
    z_sum,
    full,
    ghi,
    glo,
    load_sem,
    row_sem,
    relay,
    halo_send,
    halo_recv,
    send_sem,
    a2a_recv,
    plane_recv,
    z_recv,
    bcast_recv,
    gather_recv,
):
    narrow, wide, z_size = cfg
    slots, rows_here = cols_ref.shape
    vecs = vec_ref.shape[0]
    total = rows_here * narrow
    planes = wide // z_size
    plane = narrow * planes
    n = lax.axis_index("narrow")
    w = lax.axis_index("wide")
    z = w % z_size
    y = w // z_size
    q = y * narrow + n
    right, left = lax.rem(n + 1, narrow), lax.rem(n + narrow - 1, narrow)
    share = rows_here * LANES // wide

    def plane_device(index):
        return (index % narrow, (index // narrow) * z_size + z)

    def ring(dy, dz):
        return (n, ((y + dy) % (wide // z_size)) * z_size + (z + dz) % z_size)

    steps_y = {1: (), 2: (1,)}.get(wide // z_size, (1, wide // z_size - 1))
    circle = [(left, w), (right, w), ring(0, 1), ring(0, z_size - 1)] + [ring(dy, 0) for dy in steps_y]

    edges = [list(range(REACH)), list(range(rows_here - REACH, rows_here))]
    inner = list(range(REACH, rows_here - REACH))

    load_cols = pltpu.make_async_copy(cols_ref, cols_in, load_sem.at[0])
    load_cols.start()
    load_vec = [
        pltpu.make_async_copy(vec_ref.at[:, pl.ds(b * LANES, LANES)], ybuf.at[0, REACH + b], load_sem.at[1])
        for b in range(rows_here)
    ]
    for copy in load_vec:
        copy.start()
    load_rows = [pltpu.make_async_copy(blk_ref.at[r], blocks_in.at[r], row_sem.at[r]) for r in range(rows_here)]
    for r in edges[0] + edges[1] + inner:
        load_rows[r].start()

    barrier = pltpu.get_barrier_semaphore()
    for device in circle:
        pl.semaphore_signal(barrier, inc=1, device_id=device, device_id_type=MESH)

    load_cols.wait()
    first = n * rows_here
    for r in range(rows_here):
        for s in range(slots):
            at = cols_in[s, r] - first + REACH
            at = jnp.where(at < 0, at + total, at)
            at = jnp.where(at >= total, at - total, at)
            local_cols[r, s] = jnp.minimum(at, rows_here + 2 * REACH - 1)
    whole = ybuf.at[0, pl.ds(REACH, rows_here)]
    pltpu.make_async_copy(whole, whole, load_sem.at[1]).wait()

    pl.semaphore_wait(barrier, len(circle))

    def pass_word(j):
        for device in circle:
            pl.semaphore_signal(relay.at[j], inc=1, device_id=device, device_id_type=MESH)

    def halo_copy(j, side):
        return pltpu.make_async_remote_copy(
            src_ref=ybuf.at[j, pl.ds(rows_here if side else REACH, REACH)],
            dst_ref=ybuf.at[j, pl.ds(0 if side else rows_here + REACH, REACH)],
            send_sem=halo_send.at[j, side],
            recv_sem=halo_recv.at[j, side],
            device_id=(right if side else left, w),
            device_id_type=MESH,
        )

    halo_copy(0, 0).start()
    halo_copy(0, 1).start()
    pass_word(0)

    centre = jnp.full((vecs, LANES), (up_ref[0] + low_ref[0]) * 0.5, F32)
    inverse = 1.0 / jnp.full((vecs, LANES), (up_ref[0] - low_ref[0]) * 0.5, F32)
    keep = 1.0 - centre
    twice = 2.0 * inverse

    def put_stage(j, blocks):
        for b in blocks:
            high, low = split_pair(ybuf[j, b])
            stage[b, 0:vecs, :] = high.astype(BF16)
            stage[b, vecs : 2 * vecs, :] = low.astype(BF16)

    def prepare(r):
        load_rows[r].wait()
        for s in range(slots):
            high, low = split_pair(blocks_in[r, s])
            wbuf[r, 0:LANES, s * LANES : (s + 1) * LANES] = high.astype(BF16)
            wbuf[r, LANES : 2 * LANES, s * LANES : (s + 1) * LANES] = low.astype(BF16)

    def step(j, is_first):
        def row(r):
            x = jnp.concatenate([stage[local_cols[r, s]] for s in range(slots)], axis=1)
            o = lax.dot_general(x, wbuf[r], (((1,), (1,)), ((), ())), preferred_element_type=F32)
            prod = (o[:vecs, LANES:] + o[vecs:, :LANES]) + o[vecs:, LANES:] + o[:vecs, :LANES]
            moved = keep * ybuf[j, REACH + r] + prod
            if is_first:
                ybuf[j + 1, REACH + r] = moved * inverse
            else:
                ybuf[j + 1, REACH + r] = moved * twice - ybuf[j - 1, REACH + r]

        put_stage(j, range(REACH, REACH + rows_here))
        if is_first:
            for r in edges[0] + edges[1]:
                prepare(r)
        for side in (0, 1):
            halo_copy(j, 1 - side).wait_recv()
            put_stage(j, range(REACH + rows_here, 2 * REACH + rows_here) if side else range(REACH))
            for r in edges[side]:
                row(r)

            @pl.when(j < STEPS - 1)
            def _():
                halo_copy(j + 1, side).start()

        for r in inner:
            if is_first:
                prepare(r)
            row(r)
        pl.semaphore_wait(relay.at[j], len(circle))

        @pl.when(j < STEPS - 1)
        def _():
            pass_word(j + 1)

        for side in (0, 1):
            halo_copy(j, side).wait_send()

    def later_step(j, carry):
        step(j, False)
        return carry

    step(0, True)
    lax.fori_loop(1, STEPS, later_step, 0)

    lane = lax.broadcasted_iota(jnp.int32, (SUB, LANES), 1)

    for peer in range(wide):
        b0, off = divmod(peer * share, LANES)
        parts = []
        for h in range(HALVES):
            turn = (h * share - off) % LANES
            here = ybuf[STEPS, REACH + b0, h * SUB : (h + 1) * SUB, :]
            part = pltpu.roll(here, turn, 1) if turn else here
            if off + share > LANES:
                after = ybuf[STEPS, REACH + b0 + 1, h * SUB : (h + 1) * SUB, :]
                part2 = pltpu.roll(after, turn, 1) if turn else after
                part = jnp.where(lane < h * share + LANES - off, part, part2)
            parts.append(part)
        pack[peer] = jnp.where(lane < share, parts[0], parts[1])

    def a2a_copy(peer, slot):
        return pltpu.make_async_remote_copy(
            src_ref=pack.at[peer],
            dst_ref=arrived.at[slot],
            send_sem=send_sem.at[peer],
            recv_sem=a2a_recv.at[slot],
            device_id=(n, peer),
            device_id_type=MESH,
        )

    def a2a_start(k, carry):
        a2a_copy((w + k) % wide, w).start()
        return carry

    def a2a_wait(k, carry):
        peer = (w + k) % wide
        a2a_copy(peer, peer).wait()
        return carry

    lax.fori_loop(1, wide, a2a_start, 0)
    arrived[w] = pack[w]
    lax.fori_loop(1, wide, a2a_wait, 0)

    lane2 = lax.broadcasted_iota(jnp.int32, (HALVES * SUB, LANES), 1)

    for v in range(wide):
        tile = arrived[v]
        x = jnp.concatenate([tile, pltpu.roll(tile, LANES - share, 1)], axis=0)
        x = jnp.where(lane2 < share, x, 0.0)
        high, low = split_pair(x)
        rows = slice(v * HALVES * SUB, (v + 1) * HALVES * SUB)
        fmat[rows, :] = x
        amat[rows, 0:LANES] = (high + pltpu.roll(low, share, 1)).astype(BF16)
        amat[rows, LANES : 2 * LANES] = high.astype(BF16)
        bmat[rows, 0:LANES] = (high + pltpu.roll(high, share, 1)).astype(BF16)
        bmat[rows, LANES : 2 * LANES] = low.astype(BF16)

    side = fmat.shape[0] // LANES
    blocks_of = upper_blocks(side)
    for index, (i, j) in enumerate(blocks_of):
        gram[index * LANES : (index + 1) * LANES, :] = lax.dot_general(
            amat[i * LANES : (i + 1) * LANES, :],
            bmat[j * LANES : (j + 1) * LANES, :],
            (((1,), (1,)), ((), ())),
            preferred_element_type=F32,
        )

    chunk = gram.shape[0] // plane

    def chunk_at(index):
        return pl.ds(pl.multiple_of(index * chunk, SUB), chunk)

    def plane_copy(peer, slot):
        return pltpu.make_async_remote_copy(
            src_ref=gram.at[chunk_at(peer)],
            dst_ref=plane_in.at[slot],
            send_sem=send_sem.at[peer],
            recv_sem=plane_recv.at[slot],
            device_id=plane_device(peer),
            device_id_type=MESH,
        )

    def plane_start(k, carry):
        plane_copy((q + k) % plane, q).start()
        return carry

    def plane_wait(k, acc):
        peer = (q + k) % plane
        plane_copy(peer, peer).wait()
        return acc + plane_in[peer]

    lax.fori_loop(1, plane, plane_start, 0)
    plane_sum[...] = lax.fori_loop(1, plane, plane_wait, gram[chunk_at(q), :])

    tiles = chunk // SUB
    stride = z_size // tiles
    away = (z - n + z_size * narrow) % z_size
    owner = (away % stride == 0) & (away < stride * tiles)
    mine = jnp.minimum(away // stride, tiles - 1)

    def owner_z(t):
        return (t * stride + n) % z_size

    def z_copy(t, slot):
        return pltpu.make_async_remote_copy(
            src_ref=plane_sum.at[pl.ds(t * SUB, SUB)],
            dst_ref=z_in.at[slot],
            send_sem=send_sem.at[t],
            recv_sem=z_recv.at[slot],
            device_id=(n, y * z_size + owner_z(t)),
            device_id_type=MESH,
        )

    def tile_at(t):
        return pl.ds(pl.multiple_of(q * chunk + t * SUB, SUB), SUB)

    def bcast_copy(peer_z, t):
        return pltpu.make_async_remote_copy(
            src_ref=z_sum,
            dst_ref=full.at[tile_at(t)],
            send_sem=send_sem.at[peer_z],
            recv_sem=bcast_recv.at[t],
            device_id=(n, y * z_size + peer_z),
            device_id_type=MESH,
        )

    for t in range(tiles):

        @pl.when(owner_z(t) != z)
        def _():
            z_copy(t, z).start()

    @pl.when(owner)
    def _():
        def take(k, acc):
            peer = (z + k) % z_size
            z_copy(mine, peer).wait_recv()
            return acc + z_in[peer]

        own = plane_sum[pl.ds(pl.multiple_of(mine * SUB, SUB), SUB), :]
        z_sum[...] = lax.fori_loop(1, z_size, take, own)

    for t in range(tiles):

        @pl.when(owner_z(t) != z)
        def _():
            z_copy(t, z).wait_send()

    @pl.when(owner)
    def _():
        def give(k, carry):
            bcast_copy((z + k) % z_size, mine).start()
            return carry

        def given(k, carry):
            bcast_copy((z + k) % z_size, mine).wait_send()
            return carry

        lax.fori_loop(1, z_size, give, 0)
        full[tile_at(mine), :] = z_sum[...]
        lax.fori_loop(1, z_size, given, 0)

    for t in range(tiles):

        @pl.when(owner_z(t) != z)
        def _():
            bcast_copy(z, t).wait_recv()

    def gather_copy(peer, slot):
        return pltpu.make_async_remote_copy(
            src_ref=full.at[chunk_at(slot)],
            dst_ref=full.at[chunk_at(slot)],
            send_sem=send_sem.at[peer],
            recv_sem=gather_recv.at[slot],
            device_id=plane_device(peer),
            device_id_type=MESH,
        )

    def gather_start(k, carry):
        gather_copy((q + k) % plane, q).start()
        return carry

    def gather_wait(k, carry):
        peer = (q + k) % plane
        gather_copy(peer, peer).wait()
        return carry

    lax.fori_loop(1, plane, gather_start, 0)
    lax.fori_loop(1, plane, gather_wait, 0)

    squares = jnp.zeros((SUB, LANES), F32)
    for index, (i, j) in enumerate(blocks_of):
        block = full[index * LANES : (index + 1) * LANES, :]
        power = jnp.sum((block * block).reshape(LANES // SUB, SUB, LANES), axis=0)
        squares = squares + (power if i == j else 2.0 * power)
        high, low = split_pair(block)
        ghi[i * LANES : (i + 1) * LANES, j * LANES : (j + 1) * LANES] = high.astype(BF16)
        glo[i * LANES : (i + 1) * LANES, j * LANES : (j + 1) * LANES] = low.astype(BF16)
        if i != j:
            ghi[j * LANES : (j + 1) * LANES, i * LANES : (i + 1) * LANES] = high.T.astype(BF16)
            glo[j * LANES : (j + 1) * LANES, i * LANES : (i + 1) * LANES] = low.T.astype(BF16)

    frob = jnp.sqrt(jnp.sum(squares, keepdims=True) + 1e-06)
    scale = jnp.sqrt((total * LANES) / frob)
    main = 1.5 * scale
    cross = 0.5 * scale / frob
    fpair = amat[:, 0:LANES]
    for i in range(side):
        rows = slice(i * LANES, (i + 1) * LANES)
        zhi = jnp.dot(ghi[rows, :], fpair, preferred_element_type=F32)
        zlo = jnp.dot(glo[rows, :], fpair, preferred_element_type=F32)
        prod = (pltpu.roll(zhi, LANES - share, 1) + zlo) + zhi
        res = main * fmat[rows, :] - cross * prod
        out_ref[:, rows] = res.T[:share, :]


def on_device(cfg, vectors, blocks, columns, lower_bound, upper_bound):
    narrow, wide, z_size = cfg
    vecs, width = vectors.shape
    rows_here, slots = columns.shape
    count = vecs * wide
    side = count // LANES
    plane = narrow * (wide // z_size)
    gram_rows = len(upper_blocks(side)) * LANES
    chunk = gram_rows // plane
    ext = rows_here + 2 * REACH
    smem = pl.BlockSpec(memory_space=pltpu.SMEM)
    vmem = pl.BlockSpec(memory_space=pltpu.VMEM)
    hbm = pl.BlockSpec(memory_space=pltpu.HBM)
    dma = pltpu.SemaphoreType.DMA
    turned = pl.pallas_call(
        functools.partial(kernel_body, cfg),
        out_shape=jax.ShapeDtypeStruct((width // wide, count), F32),
        in_specs=[hbm, smem, smem, hbm, hbm],
        out_specs=vmem,
        scratch_shapes=[
            pltpu.VMEM((STEPS + 1, ext, vecs, LANES), F32),
            pltpu.VMEM((rows_here, 2 * LANES, slots * LANES), BF16),
            pltpu.VMEM((ext, 2 * vecs, LANES), BF16),
            pltpu.SMEM((rows_here, slots), jnp.int32),
            pltpu.SMEM((slots, rows_here), jnp.int32),
            pltpu.VMEM((rows_here, slots, LANES, LANES), F32),
            pltpu.VMEM((wide, SUB, LANES), F32),
            pltpu.VMEM((wide, SUB, LANES), F32),
            pltpu.VMEM((count, LANES), F32),
            pltpu.VMEM((count, 2 * LANES), BF16),
            pltpu.VMEM((count, 2 * LANES), BF16),
            pltpu.VMEM((gram_rows, LANES), F32),
            pltpu.VMEM((plane, chunk, LANES), F32),
            pltpu.VMEM((chunk, LANES), F32),
            pltpu.VMEM((z_size, SUB, LANES), F32),
            pltpu.VMEM((SUB, LANES), F32),
            pltpu.VMEM((gram_rows, LANES), F32),
            pltpu.VMEM((count, count), BF16),
            pltpu.VMEM((count, count), BF16),
            dma((2,)),
            dma((rows_here,)),
            pltpu.SemaphoreType.REGULAR((STEPS,)),
            dma((STEPS, 2)),
            dma((STEPS, 2)),
            dma((max(wide, plane, z_size),)),
            dma((wide,)),
            dma((plane,)),
            dma((z_size,)),
            dma((chunk // SUB,)),
            dma((plane,)),
        ],
        compiler_params=pltpu.CompilerParams(
            collective_id=0, has_side_effects=True, vmem_limit_bytes=67_043_328
        ),
    )(columns.T, lower_bound, upper_bound, vectors, blocks)
    return turned.T


def solution(mesh):
    cfg = (mesh.shape["narrow"], mesh.shape["wide"], Z_SIZE)
    return jax.shard_map(
        functools.partial(on_device, cfg),
        mesh=mesh,
        in_specs=(P("wide", "narrow"), P("narrow", None, None, None), P("narrow", None), P(), P()),
        out_specs=P(None, ("narrow", "wide")),
        check_vma=False,
    )
```

```python
import functools

import jax
import jax.numpy as jnp
from jax import lax
from jax.experimental import pallas as pl
from jax.experimental.pallas import tpu as pltpu
from jax.sharding import PartitionSpec as P

REACH = 3
STEPS = 8
LANES = 128
SUB = 8
HALVES = 2
Z_SIZE = 16
MESH = pl.DeviceIdType.MESH
F32 = jnp.float32
BF16 = jnp.bfloat16


def split_pair(value):
    high = value.astype(BF16).astype(F32)
    return high, value - high


def upper_blocks(count):
    return [(i, j) for i in range(count) for j in range(i, count)]


def kernel_body(
    cfg,
    cols_ref,
    low_ref,
    up_ref,
    vec_ref,
    blk_ref,
    out_ref,
    ybuf,
    wbuf,
    stage,
    local_cols,
    cols_in,
    blocks_in,
    pack,
    arrived,
    fmat,
    amat,
    bmat,
    gram,
    plane_in,
    plane_sum,
    z_in,
    z_sum,
    full,
    ghi,
    glo,
    load_sem,
    row_sem,
    relay,
    halo_send,
    halo_recv,
    send_sem,
    a2a_recv,
    plane_sent,
    plane_recv,
    z_sent,
    z_recv,
    bcast_sent,
    bcast_recv,
    gather_sent,
    gather_recv,
):
    narrow, wide, z_size = cfg
    slots, rows_here = cols_ref.shape
    vecs = vec_ref.shape[0]
    total = rows_here * narrow
    planes = wide // z_size
    plane = narrow * planes
    n = lax.axis_index("narrow")
    w = lax.axis_index("wide")
    z = w % z_size
    y = w // z_size
    q = y * narrow + n
    right, left = lax.rem(n + 1, narrow), lax.rem(n + narrow - 1, narrow)
    share = rows_here * LANES // wide

    def plane_device(index):
        return (index % narrow, (index // narrow) * z_size + z)

    def ring(dy, dz):
        return (n, ((y + dy) % (wide // z_size)) * z_size + (z + dz) % z_size)

    steps_y = {1: (), 2: (1,)}.get(wide // z_size, (1, wide // z_size - 1))
    circle = [(left, w), (right, w), ring(0, 1), ring(0, z_size - 1)] + [ring(dy, 0) for dy in steps_y]

    edges = [list(range(REACH)), list(range(rows_here - REACH, rows_here))]
    inner = list(range(REACH, rows_here - REACH))

    load_cols = pltpu.make_async_copy(cols_ref, cols_in, load_sem.at[0])
    load_cols.start()
    load_vec = [
        pltpu.make_async_copy(vec_ref.at[:, pl.ds(b * LANES, LANES)], ybuf.at[0, REACH + b], load_sem.at[1])
        for b in range(rows_here)
    ]
    for copy in load_vec:
        copy.start()
    load_rows = [pltpu.make_async_copy(blk_ref.at[r], blocks_in.at[r], row_sem.at[r]) for r in range(rows_here)]
    for r in edges[0] + edges[1] + inner:
        load_rows[r].start()

    barrier = pltpu.get_barrier_semaphore()
    for device in circle:
        pl.semaphore_signal(barrier, inc=1, device_id=device, device_id_type=MESH)

    load_cols.wait()
    first = n * rows_here
    for r in range(rows_here):
        for s in range(slots):
            at = cols_in[s, r] - first + REACH
            at = jnp.where(at < 0, at + total, at)
            at = jnp.where(at >= total, at - total, at)
            local_cols[r, s] = jnp.minimum(at, rows_here + 2 * REACH - 1)
    whole = ybuf.at[0, pl.ds(REACH, rows_here)]
    pltpu.make_async_copy(whole, whole, load_sem.at[1]).wait()

    pl.semaphore_wait(barrier, len(circle))

    def pass_word(j):
        for device in circle:
            pl.semaphore_signal(relay.at[j], inc=1, device_id=device, device_id_type=MESH)

    def halo_copy(j, side):
        return pltpu.make_async_remote_copy(
            src_ref=ybuf.at[j, pl.ds(rows_here if side else REACH, REACH)],
            dst_ref=ybuf.at[j, pl.ds(0 if side else rows_here + REACH, REACH)],
            send_sem=halo_send.at[j, side],
            recv_sem=halo_recv.at[j, side],
            device_id=(right if side else left, w),
            device_id_type=MESH,
        )

    halo_copy(0, 0).start()
    halo_copy(0, 1).start()
    pass_word(0)

    centre = jnp.full((vecs, LANES), (up_ref[0] + low_ref[0]) * 0.5, F32)
    inverse = 1.0 / jnp.full((vecs, LANES), (up_ref[0] - low_ref[0]) * 0.5, F32)
    keep = 1.0 - centre
    twice = 2.0 * inverse

    def put_stage(j, blocks):
        for b in blocks:
            high, low = split_pair(ybuf[j, b])
            stage[b, 0:vecs, :] = high.astype(BF16)
            stage[b, vecs : 2 * vecs, :] = low.astype(BF16)

    def prepare(r):
        load_rows[r].wait()
        for s in range(slots):
            high, low = split_pair(blocks_in[r, s])
            wbuf[r, 0:LANES, s * LANES : (s + 1) * LANES] = high.astype(BF16)
            wbuf[r, LANES : 2 * LANES, s * LANES : (s + 1) * LANES] = low.astype(BF16)

    def step(j, is_first):
        def row(r):
            x = jnp.concatenate([stage[local_cols[r, s]] for s in range(slots)], axis=1)
            o = lax.dot_general(x, wbuf[r], (((1,), (1,)), ((), ())), preferred_element_type=F32)
            prod = (o[:vecs, LANES:] + o[vecs:, :LANES]) + o[vecs:, LANES:] + o[:vecs, :LANES]
            moved = keep * ybuf[j, REACH + r] + prod
            if is_first:
                ybuf[j + 1, REACH + r] = moved * inverse
            else:
                ybuf[j + 1, REACH + r] = moved * twice - ybuf[j - 1, REACH + r]

        put_stage(j, range(REACH, REACH + rows_here))
        if is_first:
            for r in edges[0] + edges[1]:
                prepare(r)
        for side in (0, 1):
            halo_copy(j, 1 - side).wait_recv()
            put_stage(j, range(REACH + rows_here, 2 * REACH + rows_here) if side else range(REACH))
            for r in edges[side]:
                row(r)

            @pl.when(j < STEPS - 1)
            def _():
                halo_copy(j + 1, side).start()

        for r in inner:
            if is_first:
                prepare(r)
            row(r)
        pl.semaphore_wait(relay.at[j], len(circle))

        @pl.when(j < STEPS - 1)
        def _():
            pass_word(j + 1)

        for side in (0, 1):
            halo_copy(j, side).wait_send()

    def later_step(j, carry):
        step(j, False)
        return carry

    step(0, True)
    lax.fori_loop(1, STEPS, later_step, 0)

    lane = lax.broadcasted_iota(jnp.int32, (SUB, LANES), 1)

    for peer in range(wide):
        b0, off = divmod(peer * share, LANES)
        parts = []
        for h in range(HALVES):
            turn = (h * share - off) % LANES
            here = ybuf[STEPS, REACH + b0, h * SUB : (h + 1) * SUB, :]
            part = pltpu.roll(here, turn, 1) if turn else here
            if off + share > LANES:
                after = ybuf[STEPS, REACH + b0 + 1, h * SUB : (h + 1) * SUB, :]
                part2 = pltpu.roll(after, turn, 1) if turn else after
                part = jnp.where(lane < h * share + LANES - off, part, part2)
            parts.append(part)
        pack[peer] = jnp.where(lane < share, parts[0], parts[1])

    def a2a_copy(peer, slot):
        return pltpu.make_async_remote_copy(
            src_ref=pack.at[peer],
            dst_ref=arrived.at[slot],
            send_sem=send_sem.at[peer],
            recv_sem=a2a_recv.at[slot],
            device_id=(n, peer),
            device_id_type=MESH,
        )

    half = z_size // 2

    def far_first(i):
        away = half - (i + 1) // 2
        return jnp.where(i % 2 == 0, z_size - away, away)

    planes = wide // z_size

    def a2a_start(i, carry):
        peer = ((y + planes - 1 - i % planes) % planes) * z_size + (z + far_first(i // planes)) % z_size
        a2a_copy(peer, w).start()
        return carry

    def a2a_wait(k, carry):
        peer = (w + k) % wide
        a2a_copy(peer, peer).wait()
        return carry

    lax.fori_loop(0, wide - 1, a2a_start, 0)
    arrived[w] = pack[w]
    lax.fori_loop(1, wide, a2a_wait, 0)

    lane2 = lax.broadcasted_iota(jnp.int32, (HALVES * SUB, LANES), 1)

    for v in range(wide):
        tile = arrived[v]
        x = jnp.concatenate([tile, pltpu.roll(tile, LANES - share, 1)], axis=0)
        x = jnp.where(lane2 < share, x, 0.0)
        high, low = split_pair(x)
        rows = slice(v * HALVES * SUB, (v + 1) * HALVES * SUB)
        fmat[rows, :] = x
        amat[rows, 0:LANES] = (high + pltpu.roll(low, share, 1)).astype(BF16)
        amat[rows, LANES : 2 * LANES] = high.astype(BF16)
        bmat[rows, 0:LANES] = (high + pltpu.roll(high, share, 1)).astype(BF16)
        bmat[rows, LANES : 2 * LANES] = low.astype(BF16)

    side = fmat.shape[0] // LANES
    blocks_of = upper_blocks(side)
    for index, (i, j) in enumerate(blocks_of):
        gram[index * LANES : (index + 1) * LANES, :] = lax.dot_general(
            amat[i * LANES : (i + 1) * LANES, :],
            bmat[j * LANES : (j + 1) * LANES, :],
            (((1,), (1,)), ((), ())),
            preferred_element_type=F32,
        )

    chunk = gram.shape[0] // plane
    tiles = chunk // SUB
    stride = z_size // tiles

    def tile_rows(owner, t):
        return pl.ds(pl.multiple_of(owner * chunk + t * SUB, SUB), SUB)

    def owner_of(i):
        other = (z + far_first(i)) % z_size
        return other, (other % stride == 0) & (other < stride * tiles), jnp.minimum(other // stride, tiles - 1)

    def all_bytes(ref, sem):
        pltpu.make_async_copy(ref, ref, sem).wait()

    def plane_send(i, carry):
        _, owned, t = owner_of(i)

        @pl.when(owned)
        def _():
            def send(k, inner_carry):
                peer = (q + k) % plane
                pltpu.make_async_remote_copy(
                    src_ref=gram.at[tile_rows(peer, t)],
                    dst_ref=plane_in.at[t, k - 1],
                    send_sem=plane_sent.at[t],
                    recv_sem=plane_recv.at[t],
                    device_id=plane_device(peer),
                    device_id_type=MESH,
                ).start()
                return inner_carry

            lax.fori_loop(1, plane, send, 0)

        return carry

    lax.fori_loop(0, z_size, plane_send, 0)

    def z_copy(other, t):
        return pltpu.make_async_remote_copy(
            src_ref=plane_sum.at[t],
            dst_ref=z_in.at[(other - z + z_size) % z_size - 1],
            send_sem=z_sent.at[t],
            recv_sem=z_recv,
            device_id=(n, y * z_size + other),
            device_id_type=MESH,
        )

    def bcast_copy(other, t):
        return pltpu.make_async_remote_copy(
            src_ref=z_sum,
            dst_ref=full.at[tile_rows(q, t)],
            send_sem=bcast_sent,
            recv_sem=bcast_recv.at[t],
            device_id=(n, y * z_size + other),
            device_id_type=MESH,
        )

    def plane_reduce(i, carry):
        other, owned, t = owner_of(i)

        @pl.when(owned)
        def _():
            all_bytes(plane_in.at[t], plane_recv.at[t])
            plane_sum[t] = gram[tile_rows(q, t), :] + jnp.sum(plane_in[t], axis=0)

        @pl.when(owned & (other != z))
        def _():
            z_copy(other, t).start()

        return carry

    lax.fori_loop(0, z_size, plane_reduce, 0)

    _, owner_here, mine = owner_of(z_size - 1)

    @pl.when(owner_here)
    def _():
        all_bytes(z_in, z_recv)
        z_sum[...] = plane_sum[mine] + jnp.sum(z_in[...], axis=0)

        def give(i, carry):
            bcast_copy((z + far_first(i)) % z_size, mine).start()
            return carry

        lax.fori_loop(0, z_size - 1, give, 0)
        full[tile_rows(q, mine), :] = z_sum[...]

    def gather_send(i, carry):
        other, owned, t = owner_of(z_size - 1 - i)

        @pl.when(owned & (other != z))
        def _():
            bcast_copy(z, t).wait_recv()

        @pl.when(owned)
        def _():
            def send(k, inner_carry):
                peer = (q + k) % plane
                pltpu.make_async_remote_copy(
                    src_ref=full.at[tile_rows(q, t)],
                    dst_ref=full.at[tile_rows(q, t)],
                    send_sem=gather_sent.at[t],
                    recv_sem=gather_recv.at[t],
                    device_id=plane_device(peer),
                    device_id_type=MESH,
                ).start()
                return inner_carry

            lax.fori_loop(1, plane, send, 0)

        return carry

    lax.fori_loop(0, z_size, gather_send, 0)

    for t in range(tiles):
        all_bytes(plane_in.at[t], gather_recv.at[t])

    squares = jnp.zeros((SUB, LANES), F32)
    for index, (i, j) in enumerate(blocks_of):
        block = full[index * LANES : (index + 1) * LANES, :]
        power = jnp.sum((block * block).reshape(LANES // SUB, SUB, LANES), axis=0)
        squares = squares + (power if i == j else 2.0 * power)
        high, low = split_pair(block)
        ghi[i * LANES : (i + 1) * LANES, j * LANES : (j + 1) * LANES] = high.astype(BF16)
        glo[i * LANES : (i + 1) * LANES, j * LANES : (j + 1) * LANES] = low.astype(BF16)
        if i != j:
            ghi[j * LANES : (j + 1) * LANES, i * LANES : (i + 1) * LANES] = high.T.astype(BF16)
            glo[j * LANES : (j + 1) * LANES, i * LANES : (i + 1) * LANES] = low.T.astype(BF16)

    frob = jnp.sqrt(jnp.sum(squares, keepdims=True) + 1e-06)
    scale = jnp.sqrt((total * LANES) / frob)
    main = 1.5 * scale
    cross = 0.5 * scale / frob
    fpair = amat[:, 0:LANES]
    for i in range(side):
        rows = slice(i * LANES, (i + 1) * LANES)
        zhi = jnp.dot(ghi[rows, :], fpair, preferred_element_type=F32)
        zlo = jnp.dot(glo[rows, :], fpair, preferred_element_type=F32)
        prod = (pltpu.roll(zhi, LANES - share, 1) + zlo) + zhi
        res = main * fmat[rows, :] - cross * prod
        out_ref[:, rows] = res.T[:share, :]

    for t in range(tiles):
        all_bytes(plane_in.at[t], plane_sent.at[t])
        all_bytes(plane_in.at[t], gather_sent.at[t])

    def z_drain(i, carry):
        other, owned, t = owner_of(i)

        @pl.when(owned & (other != z))
        def _():
            z_copy(other, t).wait_send()

        return carry

    lax.fori_loop(0, z_size, z_drain, 0)

    @pl.when(owner_here)
    def _():
        all_bytes(z_in, bcast_sent)


def on_device(cfg, vectors, blocks, columns, lower_bound, upper_bound):
    narrow, wide, z_size = cfg
    vecs, width = vectors.shape
    rows_here, slots = columns.shape
    count = vecs * wide
    side = count // LANES
    plane = narrow * (wide // z_size)
    gram_rows = len(upper_blocks(side)) * LANES
    tiles = gram_rows // plane // SUB
    ext = rows_here + 2 * REACH
    smem = pl.BlockSpec(memory_space=pltpu.SMEM)
    vmem = pl.BlockSpec(memory_space=pltpu.VMEM)
    hbm = pl.BlockSpec(memory_space=pltpu.HBM)
    dma = pltpu.SemaphoreType.DMA
    turned = pl.pallas_call(
        functools.partial(kernel_body, cfg),
        out_shape=jax.ShapeDtypeStruct((width // wide, count), F32),
        in_specs=[hbm, smem, smem, hbm, hbm],
        out_specs=vmem,
        scratch_shapes=[
            pltpu.VMEM((STEPS + 1, ext, vecs, LANES), F32),
            pltpu.VMEM((rows_here, 2 * LANES, slots * LANES), BF16),
            pltpu.VMEM((ext, 2 * vecs, LANES), BF16),
            pltpu.SMEM((rows_here, slots), jnp.int32),
            pltpu.SMEM((slots, rows_here), jnp.int32),
            pltpu.VMEM((rows_here, slots, LANES, LANES), F32),
            pltpu.VMEM((wide, SUB, LANES), F32),
            pltpu.VMEM((wide, SUB, LANES), F32),
            pltpu.VMEM((count, LANES), F32),
            pltpu.VMEM((count, 2 * LANES), BF16),
            pltpu.VMEM((count, 2 * LANES), BF16),
            pltpu.VMEM((gram_rows, LANES), F32),
            pltpu.VMEM((tiles, plane - 1, SUB, LANES), F32),
            pltpu.VMEM((tiles, SUB, LANES), F32),
            pltpu.VMEM((z_size - 1, SUB, LANES), F32),
            pltpu.VMEM((SUB, LANES), F32),
            pltpu.VMEM((gram_rows, LANES), F32),
            pltpu.VMEM((count, count), BF16),
            pltpu.VMEM((count, count), BF16),
            dma((2,)),
            dma((rows_here,)),
            pltpu.SemaphoreType.REGULAR((STEPS,)),
            dma((STEPS, 2)),
            dma((STEPS, 2)),
            dma((wide,)),
            dma((wide,)),
            dma((tiles,)),
            dma((tiles,)),
            dma((tiles,)),
            dma,
            dma,
            dma((tiles,)),
            dma((tiles,)),
            dma((tiles,)),
        ],
        compiler_params=pltpu.CompilerParams(
            collective_id=0, has_side_effects=True, vmem_limit_bytes=67_043_328
        ),
    )(columns.T, lower_bound, upper_bound, vectors, blocks)
    return turned.T


def solution(mesh):
    cfg = (mesh.shape["narrow"], mesh.shape["wide"], Z_SIZE)
    return jax.shard_map(
        functools.partial(on_device, cfg),
        mesh=mesh,
        in_specs=(P("wide", "narrow"), P("narrow", None, None, None), P("narrow", None), P(), P()),
        out_specs=P(None, ("narrow", "wide")),
        check_vma=False,
    )
```

```python
import functools

import jax
import jax.numpy as jnp
from jax import lax
from jax.experimental import pallas as pl
from jax.experimental.pallas import tpu as pltpu
from jax.sharding import PartitionSpec as P

REACH = 3
STEPS = 8
LANES = 128
SUB = 8
HALVES = 2
Z_SIZE = 16
MESH = pl.DeviceIdType.MESH
F32 = jnp.float32
BF16 = jnp.bfloat16


def split_pair(value):
    high = value.astype(BF16).astype(F32)
    return high, value - high


def upper_blocks(count):
    return [(i, j) for i in range(count) for j in range(i, count)]


def kernel_body(
    cfg,
    cols_ref,
    low_ref,
    up_ref,
    vec_ref,
    blk_ref,
    out_ref,
    ybuf,
    wbuf,
    stage,
    local_cols,
    cols_in,
    blocks_in,
    pack,
    arrived,
    fmat,
    amat,
    bmat,
    gram,
    plane_in,
    plane_sum,
    z_in,
    z_sum,
    full,
    ghi,
    glo,
    load_sem,
    row_sem,
    relay,
    halo_send,
    halo_recv,
    send_sem,
    a2a_recv,
    plane_sent,
    plane_recv,
    z_sent,
    z_recv,
    bcast_sent,
    bcast_recv,
    gather_sent,
    gather_recv,
):
    narrow, wide, z_size = cfg
    slots, rows_here = cols_ref.shape
    vecs = vec_ref.shape[0]
    total = rows_here * narrow
    planes = wide // z_size
    plane = narrow * planes
    n = lax.axis_index("narrow")
    w = lax.axis_index("wide")
    z = w % z_size
    y = w // z_size
    q = y * narrow + n
    right, left = lax.rem(n + 1, narrow), lax.rem(n + narrow - 1, narrow)
    share = rows_here * LANES // wide

    planes = wide // z_size
    size_x, size_y = narrow // 4, planes * 2
    x, full_y, core = n // 4, y * 2 + lax.rem(n // 2, 2), lax.rem(n, 2)

    def hops(offset):
        return min(offset[0], size_x - offset[0]) + min(offset[1], size_y - offset[1])

    offsets = [(dx, dy, dc) for dx in range(size_x) for dy in range(size_y) for dc in range(2)][1:]
    plane_peers = []
    for dx, dy, dc in sorted(offsets, key=hops, reverse=True):
        peer_y = lax.rem(full_y + dy, size_y)
        peer_n = lax.rem(x + dx, size_x) * 4 + lax.rem(peer_y, 2) * 2 + lax.rem(core + dc, 2)
        plane_peers.append((peer_y // 2 * narrow + peer_n, (peer_n, peer_y // 2 * z_size + z)))

    def ring(dy, dz):
        return (n, ((y + dy) % (wide // z_size)) * z_size + (z + dz) % z_size)

    steps_y = {1: (), 2: (1,)}.get(wide // z_size, (1, wide // z_size - 1))
    circle = [(left, w), (right, w), ring(0, 1), ring(0, z_size - 1)] + [ring(dy, 0) for dy in steps_y]

    edges = [list(range(REACH)), list(range(rows_here - REACH, rows_here))]
    inner = list(range(REACH, rows_here - REACH))

    load_cols = pltpu.make_async_copy(cols_ref, cols_in, load_sem.at[0])
    load_cols.start()
    load_vec = [
        pltpu.make_async_copy(vec_ref.at[:, pl.ds(b * LANES, LANES)], ybuf.at[0, REACH + b], load_sem.at[1])
        for b in range(rows_here)
    ]
    for copy in load_vec:
        copy.start()
    load_rows = [pltpu.make_async_copy(blk_ref.at[r], blocks_in.at[r], row_sem.at[r]) for r in range(rows_here)]
    for r in edges[0] + edges[1] + inner:
        load_rows[r].start()

    barrier = pltpu.get_barrier_semaphore()
    for device in circle:
        pl.semaphore_signal(barrier, inc=1, device_id=device, device_id_type=MESH)

    whole = ybuf.at[0, pl.ds(REACH, rows_here)]
    pltpu.make_async_copy(whole, whole, load_sem.at[1]).wait()

    pl.semaphore_wait(barrier, len(circle))

    def pass_word(j):
        for device in circle:
            pl.semaphore_signal(relay.at[j], inc=1, device_id=device, device_id_type=MESH)

    def halo_copy(j, side):
        return pltpu.make_async_remote_copy(
            src_ref=ybuf.at[j, pl.ds(rows_here if side else REACH, REACH)],
            dst_ref=ybuf.at[j, pl.ds(0 if side else rows_here + REACH, REACH)],
            send_sem=halo_send.at[j, side],
            recv_sem=halo_recv.at[j, side],
            device_id=(right if side else left, w),
            device_id_type=MESH,
        )

    halo_copy(0, 0).start()
    halo_copy(0, 1).start()
    pass_word(0)

    load_cols.wait()
    first = n * rows_here
    for r in range(rows_here):
        for s in range(slots):
            at = cols_in[s, r] - first + REACH
            at = jnp.where(at < 0, at + total, at)
            at = jnp.where(at >= total, at - total, at)
            local_cols[r, s] = jnp.minimum(at, rows_here + 2 * REACH - 1)

    centre = jnp.full((vecs, LANES), (up_ref[0] + low_ref[0]) * 0.5, F32)
    inverse = 1.0 / jnp.full((vecs, LANES), (up_ref[0] - low_ref[0]) * 0.5, F32)
    keep = 1.0 - centre
    twice = 2.0 * inverse

    def put_stage(j, blocks):
        for b in blocks:
            high, low = split_pair(ybuf[j, b])
            stage[b, 0:vecs, :] = high.astype(BF16)
            stage[b, vecs : 2 * vecs, :] = low.astype(BF16)

    def prepare(r):
        load_rows[r].wait()
        for s in range(slots):
            high, low = split_pair(blocks_in[r, s])
            wbuf[r, 0:LANES, s * LANES : (s + 1) * LANES] = high.astype(BF16)
            wbuf[r, LANES : 2 * LANES, s * LANES : (s + 1) * LANES] = low.astype(BF16)

    lane = lax.broadcasted_iota(jnp.int32, (SUB, LANES), 1)

    def pack_one(peer):
        b0, off = divmod(peer * share, LANES)
        parts = []
        for h in range(HALVES):
            turn = (h * share - off) % LANES
            here = ybuf[STEPS, REACH + b0, h * SUB : (h + 1) * SUB, :]
            part = pltpu.roll(here, turn, 1) if turn else here
            if off + share > LANES:
                after = ybuf[STEPS, REACH + b0 + 1, h * SUB : (h + 1) * SUB, :]
                part2 = pltpu.roll(after, turn, 1) if turn else after
                part = jnp.where(lane < h * share + LANES - off, part, part2)
            parts.append(part)
        pack[peer] = jnp.where(lane < share, parts[0], parts[1])

    def a2a_copy(peer, slot):
        return pltpu.make_async_remote_copy(
            src_ref=pack.at[peer],
            dst_ref=arrived.at[slot],
            send_sem=send_sem.at[peer],
            recv_sem=a2a_recv.at[slot],
            device_id=(n, peer),
            device_id_type=MESH,
        )

    def send_packed(peers):
        for peer in peers:
            pack_one(peer)
        for peer in peers:

            @pl.when(w != peer)
            def _():
                a2a_copy(peer, w).start()

    def last_block(peer):
        return (peer * share + share - 1) // LANES

    edge_peers = [[p for p in range(wide) if p * share // LANES < REACH], []]
    inner_peers = [p for p in range(wide) if p * share // LANES >= REACH and last_block(p) < rows_here - REACH]
    edge_peers[1] = [p for p in range(wide) if p not in edge_peers[0] + inner_peers]
    assert all(last_block(p) < rows_here - REACH for p in edge_peers[0])

    def step(j, is_first, is_last):
        def row(r):
            x = jnp.concatenate([stage[local_cols[r, s]] for s in range(slots)], axis=1)
            o = lax.dot_general(x, wbuf[r], (((1,), (1,)), ((), ())), preferred_element_type=F32)
            prod = (o[:vecs, LANES:] + o[vecs:, :LANES]) + o[vecs:, LANES:] + o[:vecs, :LANES]
            moved = keep * ybuf[j, REACH + r] + prod
            if is_first:
                ybuf[j + 1, REACH + r] = moved * inverse
            else:
                ybuf[j + 1, REACH + r] = moved * twice - ybuf[j - 1, REACH + r]

        put_stage(j, range(REACH, REACH + rows_here))
        if is_first:
            for r in edges[0] + edges[1]:
                prepare(r)
        if is_last:
            for r in inner:
                row(r)
            pl.semaphore_wait(relay.at[j], len(circle))
            send_packed(inner_peers)
        for side in (0, 1):
            halo_copy(j, 1 - side).wait_recv()
            put_stage(j, range(REACH + rows_here, 2 * REACH + rows_here) if side else range(REACH))
            for r in edges[side]:
                row(r)
            if is_last:
                send_packed(edge_peers[side])
            else:
                halo_copy(j + 1, side).start()

        if not is_last:
            for r in inner:
                if is_first:
                    prepare(r)
                row(r)
            pl.semaphore_wait(relay.at[j], len(circle))
            pass_word(j + 1)

        for side in (0, 1):
            halo_copy(j, side).wait_send()

    def later_step(j, carry):
        step(j, False, False)
        return carry

    step(0, True, False)
    lax.fori_loop(1, STEPS - 1, later_step, 0)
    step(STEPS - 1, False, True)
    arrived[w] = pack[w]

    half = z_size // 2

    def far_first(i):
        away = half - (i + 1) // 2
        return jnp.where(i % 2 == 0, z_size - away, away)

    def a2a_wait(k, carry):
        peer = (w + k) % wide
        a2a_copy(peer, peer).wait()
        return carry

    lax.fori_loop(1, wide, a2a_wait, 0)

    lane2 = lax.broadcasted_iota(jnp.int32, (HALVES * SUB, LANES), 1)

    for v in range(wide):
        tile = arrived[v]
        x = jnp.concatenate([tile, pltpu.roll(tile, LANES - share, 1)], axis=0)
        x = jnp.where(lane2 < share, x, 0.0)
        high, low = split_pair(x)
        rows = slice(v * HALVES * SUB, (v + 1) * HALVES * SUB)
        fmat[rows, :] = x
        amat[rows, 0:LANES] = (high + pltpu.roll(low, share, 1)).astype(BF16)
        amat[rows, LANES : 2 * LANES] = high.astype(BF16)
        bmat[rows, 0:LANES] = (high + pltpu.roll(high, share, 1)).astype(BF16)
        bmat[rows, LANES : 2 * LANES] = low.astype(BF16)

    side = fmat.shape[0] // LANES
    blocks_of = upper_blocks(side)
    for index, (i, j) in enumerate(blocks_of):
        gram[index * LANES : (index + 1) * LANES, :] = lax.dot_general(
            amat[i * LANES : (i + 1) * LANES, :],
            bmat[j * LANES : (j + 1) * LANES, :],
            (((1,), (1,)), ((), ())),
            preferred_element_type=F32,
        )

    chunk = gram.shape[0] // plane
    tiles = chunk // SUB
    stride = z_size // tiles

    def tile_rows(owner, t):
        return pl.ds(pl.multiple_of(owner * chunk + t * SUB, SUB), SUB)

    def owner_of(i):
        other = (z + far_first(i)) % z_size
        return other, (other % stride == 0) & (other < stride * tiles), jnp.minimum(other // stride, tiles - 1)

    def all_bytes(ref, sem):
        pltpu.make_async_copy(ref, ref, sem).wait()

    def plane_send(i, carry):
        _, owned, t = owner_of(i)

        @pl.when(owned)
        def _():
            for k, (peer, device) in enumerate(plane_peers):
                pltpu.make_async_remote_copy(
                    src_ref=gram.at[tile_rows(peer, t)],
                    dst_ref=plane_in.at[t, k],
                    send_sem=plane_sent.at[t],
                    recv_sem=plane_recv.at[t],
                    device_id=device,
                    device_id_type=MESH,
                ).start()

        return carry

    lax.fori_loop(0, z_size, plane_send, 0)

    def z_copy(other, t):
        return pltpu.make_async_remote_copy(
            src_ref=plane_sum.at[t],
            dst_ref=z_in.at[(other - z + z_size) % z_size - 1],
            send_sem=z_sent.at[t],
            recv_sem=z_recv,
            device_id=(n, y * z_size + other),
            device_id_type=MESH,
        )

    def bcast_copy(other, t):
        return pltpu.make_async_remote_copy(
            src_ref=z_sum,
            dst_ref=full.at[tile_rows(q, t)],
            send_sem=bcast_sent,
            recv_sem=bcast_recv.at[t],
            device_id=(n, y * z_size + other),
            device_id_type=MESH,
        )

    def plane_reduce(i, carry):
        other, owned, t = owner_of(i)

        @pl.when(owned)
        def _():
            all_bytes(plane_in.at[t], plane_recv.at[t])
            plane_sum[t] = gram[tile_rows(q, t), :] + jnp.sum(plane_in[t], axis=0)

        @pl.when(owned & (other != z))
        def _():
            z_copy(other, t).start()

        return carry

    lax.fori_loop(0, z_size, plane_reduce, 0)

    _, owner_here, mine = owner_of(z_size - 1)

    @pl.when(owner_here)
    def _():
        all_bytes(z_in, z_recv)
        z_sum[...] = plane_sum[mine] + jnp.sum(z_in[...], axis=0)

        def give(i, carry):
            bcast_copy((z + far_first(i)) % z_size, mine).start()
            return carry

        lax.fori_loop(0, z_size - 1, give, 0)
        full[tile_rows(q, mine), :] = z_sum[...]

    def gather_send(i, carry):
        other, owned, t = owner_of(z_size - 1 - i)

        @pl.when(owned & (other != z))
        def _():
            bcast_copy(z, t).wait_recv()

        @pl.when(owned)
        def _():
            for _, device in plane_peers:
                pltpu.make_async_remote_copy(
                    src_ref=full.at[tile_rows(q, t)],
                    dst_ref=full.at[tile_rows(q, t)],
                    send_sem=gather_sent.at[t],
                    recv_sem=gather_recv.at[t],
                    device_id=device,
                    device_id_type=MESH,
                ).start()

        return carry

    lax.fori_loop(0, z_size, gather_send, 0)

    for t in range(tiles):
        all_bytes(plane_in.at[t], gather_recv.at[t])

    squares = jnp.zeros((SUB, LANES), F32)
    for index, (i, j) in enumerate(blocks_of):
        block = full[index * LANES : (index + 1) * LANES, :]
        power = jnp.sum((block * block).reshape(LANES // SUB, SUB, LANES), axis=0)
        squares = squares + (power if i == j else 2.0 * power)
        high, low = split_pair(block)
        ghi[i * LANES : (i + 1) * LANES, j * LANES : (j + 1) * LANES] = high.astype(BF16)
        glo[i * LANES : (i + 1) * LANES, j * LANES : (j + 1) * LANES] = low.astype(BF16)
        if i != j:
            ghi[j * LANES : (j + 1) * LANES, i * LANES : (i + 1) * LANES] = high.T.astype(BF16)
            glo[j * LANES : (j + 1) * LANES, i * LANES : (i + 1) * LANES] = low.T.astype(BF16)

    frob = jnp.sqrt(jnp.sum(squares, keepdims=True) + 1e-06)
    scale = jnp.sqrt((total * LANES) / frob)
    main = 1.5 * scale
    cross = 0.5 * scale / frob
    fpair = amat[:, 0:LANES]
    for i in range(side):
        rows = slice(i * LANES, (i + 1) * LANES)
        zhi = jnp.dot(ghi[rows, :], fpair, preferred_element_type=F32)
        zlo = jnp.dot(glo[rows, :], fpair, preferred_element_type=F32)
        prod = (pltpu.roll(zhi, LANES - share, 1) + zlo) + zhi
        res = main * fmat[rows, :] - cross * prod
        out_ref[:, rows] = res.T[:share, :]

    for t in range(tiles):
        all_bytes(plane_in.at[t], plane_sent.at[t])
        all_bytes(plane_in.at[t], gather_sent.at[t])

    def z_drain(i, carry):
        other, owned, t = owner_of(i)

        @pl.when(owned & (other != z))
        def _():
            z_copy(other, t).wait_send()

        return carry

    lax.fori_loop(0, z_size, z_drain, 0)

    @pl.when(owner_here)
    def _():
        all_bytes(z_in, bcast_sent)


def on_device(cfg, vectors, blocks, columns, lower_bound, upper_bound):
    narrow, wide, z_size = cfg
    vecs, width = vectors.shape
    rows_here, slots = columns.shape
    count = vecs * wide
    side = count // LANES
    plane = narrow * (wide // z_size)
    gram_rows = len(upper_blocks(side)) * LANES
    tiles = gram_rows // plane // SUB
    ext = rows_here + 2 * REACH
    smem = pl.BlockSpec(memory_space=pltpu.SMEM)
    vmem = pl.BlockSpec(memory_space=pltpu.VMEM)
    hbm = pl.BlockSpec(memory_space=pltpu.HBM)
    dma = pltpu.SemaphoreType.DMA
    turned = pl.pallas_call(
        functools.partial(kernel_body, cfg),
        out_shape=jax.ShapeDtypeStruct((width // wide, count), F32),
        in_specs=[hbm, smem, smem, hbm, hbm],
        out_specs=vmem,
        scratch_shapes=[
            pltpu.VMEM((STEPS + 1, ext, vecs, LANES), F32),
            pltpu.VMEM((rows_here, 2 * LANES, slots * LANES), BF16),
            pltpu.VMEM((ext, 2 * vecs, LANES), BF16),
            pltpu.SMEM((rows_here, slots), jnp.int32),
            pltpu.SMEM((slots, rows_here), jnp.int32),
            pltpu.VMEM((rows_here, slots, LANES, LANES), F32),
            pltpu.VMEM((wide, SUB, LANES), F32),
            pltpu.VMEM((wide, SUB, LANES), F32),
            pltpu.VMEM((count, LANES), F32),
            pltpu.VMEM((count, 2 * LANES), BF16),
            pltpu.VMEM((count, 2 * LANES), BF16),
            pltpu.VMEM((gram_rows, LANES), F32),
            pltpu.VMEM((tiles, plane - 1, SUB, LANES), F32),
            pltpu.VMEM((tiles, SUB, LANES), F32),
            pltpu.VMEM((z_size - 1, SUB, LANES), F32),
            pltpu.VMEM((SUB, LANES), F32),
            pltpu.VMEM((gram_rows, LANES), F32),
            pltpu.VMEM((count, count), BF16),
            pltpu.VMEM((count, count), BF16),
            dma((2,)),
            dma((rows_here,)),
            pltpu.SemaphoreType.REGULAR((STEPS,)),
            dma((STEPS, 2)),
            dma((STEPS, 2)),
            dma((wide,)),
            dma((wide,)),
            dma((tiles,)),
            dma((tiles,)),
            dma((tiles,)),
            dma,
            dma,
            dma((tiles,)),
            dma((tiles,)),
            dma((tiles,)),
        ],
        compiler_params=pltpu.CompilerParams(
            collective_id=0, has_side_effects=True, vmem_limit_bytes=67_043_328
        ),
    )(columns.T, lower_bound, upper_bound, vectors, blocks)
    return turned.T


def solution(mesh):
    cfg = (mesh.shape["narrow"], mesh.shape["wide"], Z_SIZE)
    return jax.shard_map(
        functools.partial(on_device, cfg),
        mesh=mesh,
        in_specs=(P("wide", "narrow"), P("narrow", None, None, None), P("narrow", None), P(), P()),
        out_specs=P(None, ("narrow", "wide")),
        check_vma=False,
    )
```

```python
import functools

import jax
import jax.numpy as jnp
from jax import lax
from jax.experimental import pallas as pl
from jax.experimental.pallas import tpu as pltpu
from jax.sharding import PartitionSpec as P

REACH = 3
STEPS = 8
LANES = 128
SUB = 8
HALVES = 2
Z_SIZE = 16
MESH = pl.DeviceIdType.MESH
F32 = jnp.float32
BF16 = jnp.bfloat16


def split_pair(value):
    high = value.astype(BF16).astype(F32)
    return high, value - high


def upper_blocks(count):
    return [(i, j) for i in range(count) for j in range(i, count)]


def kernel_body(
    cfg,
    cols_ref,
    low_ref,
    up_ref,
    vec_ref,
    blk_ref,
    out_ref,
    ybuf,
    wbuf,
    stage,
    whalo,
    partial,
    local_cols,
    own_cols,
    cols_in,
    blocks_in,
    pack,
    arrived,
    fmat,
    amat,
    bmat,
    gram,
    plane_in,
    plane_sum,
    z_in,
    z_sum,
    full,
    ghi,
    glo,
    load_sem,
    row_sem,
    relay,
    halo_send,
    halo_recv,
    send_sem,
    a2a_recv,
    plane_sent,
    plane_recv,
    z_sent,
    z_recv,
    bcast_sent,
    bcast_recv,
    gather_sent,
    gather_recv,
):
    narrow, wide, z_size = cfg
    slots, rows_here = cols_ref.shape
    vecs = vec_ref.shape[0]
    total = rows_here * narrow
    planes = wide // z_size
    plane = narrow * planes
    n = lax.axis_index("narrow")
    w = lax.axis_index("wide")
    z = w % z_size
    y = w // z_size
    q = y * narrow + n
    right, left = lax.rem(n + 1, narrow), lax.rem(n + narrow - 1, narrow)
    share = rows_here * LANES // wide

    planes = wide // z_size
    size_x, size_y = narrow // 4, planes * 2
    x, full_y, core = n // 4, y * 2 + lax.rem(n // 2, 2), lax.rem(n, 2)

    def hops(offset):
        return min(offset[0], size_x - offset[0]) + min(offset[1], size_y - offset[1])

    offsets = [(dx, dy, dc) for dx in range(size_x) for dy in range(size_y) for dc in range(2)][1:]
    plane_peers = []
    for dx, dy, dc in sorted(offsets, key=hops, reverse=True):
        peer_y = lax.rem(full_y + dy, size_y)
        peer_n = lax.rem(x + dx, size_x) * 4 + lax.rem(peer_y, 2) * 2 + lax.rem(core + dc, 2)
        plane_peers.append((peer_y // 2 * narrow + peer_n, (peer_n, peer_y // 2 * z_size + z)))

    def ring(dy, dz):
        return (n, ((y + dy) % (wide // z_size)) * z_size + (z + dz) % z_size)

    steps_y = {1: (), 2: (1,)}.get(wide // z_size, (1, wide // z_size - 1))
    circle = [(left, w), (right, w), ring(0, 1), ring(0, z_size - 1)] + [ring(dy, 0) for dy in steps_y]

    edges = [list(range(REACH)), list(range(rows_here - REACH, rows_here))]
    inner = list(range(REACH, rows_here - REACH))

    load_cols = pltpu.make_async_copy(cols_ref, cols_in, load_sem.at[0])
    load_cols.start()
    load_vec = [
        pltpu.make_async_copy(vec_ref.at[:, pl.ds(b * LANES, LANES)], ybuf.at[0, REACH + b], load_sem.at[1])
        for b in range(rows_here)
    ]
    for copy in load_vec:
        copy.start()
    load_rows = [pltpu.make_async_copy(blk_ref.at[r], blocks_in.at[r], row_sem.at[r]) for r in range(rows_here)]
    for r in edges[0] + edges[1] + inner:
        load_rows[r].start()

    barrier = pltpu.get_barrier_semaphore()
    for device in circle:
        pl.semaphore_signal(barrier, inc=1, device_id=device, device_id_type=MESH)

    whole = ybuf.at[0, pl.ds(REACH, rows_here)]
    pltpu.make_async_copy(whole, whole, load_sem.at[1]).wait()

    pl.semaphore_wait(barrier, len(circle))

    def pass_word(j):
        for device in circle:
            pl.semaphore_signal(relay.at[j], inc=1, device_id=device, device_id_type=MESH)

    def halo_copy(j, side):
        return pltpu.make_async_remote_copy(
            src_ref=ybuf.at[j, pl.ds(rows_here if side else REACH, REACH)],
            dst_ref=ybuf.at[j, pl.ds(0 if side else rows_here + REACH, REACH)],
            send_sem=halo_send.at[j, side],
            recv_sem=halo_recv.at[j, side],
            device_id=(right if side else left, w),
            device_id_type=MESH,
        )

    halo_copy(0, 0).start()
    halo_copy(0, 1).start()
    pass_word(0)

    load_cols.wait()
    first = n * rows_here
    for r in range(rows_here):
        for s in range(slots):
            at = cols_in[s, r] - first + REACH
            at = jnp.where(at < 0, at + total, at)
            at = jnp.where(at >= total, at - total, at)
            local_cols[r, s] = jnp.minimum(at, rows_here + 2 * REACH - 1)
            at_home = (at >= REACH) & (at < REACH + rows_here)
            own_cols[r, s] = jnp.where(at_home, at, rows_here + 2 * REACH)

    centre = jnp.full((vecs, LANES), (up_ref[0] + low_ref[0]) * 0.5, F32)
    inverse = 1.0 / jnp.full((vecs, LANES), (up_ref[0] - low_ref[0]) * 0.5, F32)
    keep = 1.0 - centre
    twice = 2.0 * inverse

    def put_stage(j, blocks):
        for b in blocks:
            high, low = split_pair(ybuf[j, b])
            stage[b, 0:vecs, :] = high.astype(BF16)
            stage[b, vecs : 2 * vecs, :] = low.astype(BF16)

    stage[rows_here + 2 * REACH] = jnp.zeros((2 * vecs, LANES), BF16)

    def halo_of(side, k):
        return range(rows_here + REACH, rows_here + REACH + k + 1) if side else range(k, REACH)

    def prepare(r):
        load_rows[r].wait()
        for s in range(slots):
            high, low = split_pair(blocks_in[r, s])
            wbuf[r, 0:LANES, s * LANES : (s + 1) * LANES] = high.astype(BF16)
            wbuf[r, LANES : 2 * LANES, s * LANES : (s + 1) * LANES] = low.astype(BF16)

    def prepare_halo(side, k):
        r = edges[side][k]
        for i, b in enumerate(halo_of(side, k)):
            total_block = jnp.zeros((LANES, LANES), F32)
            for s in range(slots):
                total_block = total_block + jnp.where(local_cols[r, s] == b, 1.0, 0.0).astype(F32) * blocks_in[r, s]
            high, low = split_pair(total_block)
            whalo[side, k, 0:LANES, i * LANES : (i + 1) * LANES] = high.astype(BF16)
            whalo[side, k, LANES : 2 * LANES, i * LANES : (i + 1) * LANES] = low.astype(BF16)

    lane = lax.broadcasted_iota(jnp.int32, (SUB, LANES), 1)

    def pack_one(peer):
        b0, off = divmod(peer * share, LANES)
        parts = []
        for h in range(HALVES):
            turn = (h * share - off) % LANES
            here = ybuf[STEPS, REACH + b0, h * SUB : (h + 1) * SUB, :]
            part = pltpu.roll(here, turn, 1) if turn else here
            if off + share > LANES:
                after = ybuf[STEPS, REACH + b0 + 1, h * SUB : (h + 1) * SUB, :]
                part2 = pltpu.roll(after, turn, 1) if turn else after
                part = jnp.where(lane < h * share + LANES - off, part, part2)
            parts.append(part)
        pack[peer] = jnp.where(lane < share, parts[0], parts[1])

    def a2a_copy(peer, slot):
        return pltpu.make_async_remote_copy(
            src_ref=pack.at[peer],
            dst_ref=arrived.at[slot],
            send_sem=send_sem.at[peer],
            recv_sem=a2a_recv.at[slot],
            device_id=(n, peer),
            device_id_type=MESH,
        )

    def send_packed(peers):
        for peer in peers:
            pack_one(peer)
        for peer in peers:

            @pl.when(w != peer)
            def _():
                a2a_copy(peer, w).start()

    def last_block(peer):
        return (peer * share + share - 1) // LANES

    edge_peers = [[p for p in range(wide) if p * share // LANES < REACH], []]
    inner_peers = [p for p in range(wide) if p * share // LANES >= REACH and last_block(p) < rows_here - REACH]
    edge_peers[1] = [p for p in range(wide) if p not in edge_peers[0] + inner_peers]
    assert all(last_block(p) < rows_here - REACH for p in edge_peers[0])

    def step(j, is_first, is_last):
        def gathered(o):
            return (o[:vecs, LANES:] + o[vecs:, :LANES]) + o[vecs:, LANES:] + o[:vecs, :LANES]

        def product(r):
            x = jnp.concatenate([stage[own_cols[r, s]] for s in range(slots)], axis=1)
            return gathered(lax.dot_general(x, wbuf[r], (((1,), (1,)), ((), ())), preferred_element_type=F32))

        def row(r):
            moved = keep * ybuf[j, REACH + r] + product(r)
            if is_first:
                ybuf[j + 1, REACH + r] = moved * inverse
            else:
                ybuf[j + 1, REACH + r] = moved * twice - ybuf[j - 1, REACH + r]

        def edge_own(side, k):
            r = edges[side][k]
            moved = keep * ybuf[j, REACH + r] + product(r)
            partial[side, k] = moved * inverse if is_first else moved * twice - ybuf[j - 1, REACH + r]

        def edge_rest(side, k):
            places = halo_of(side, k)
            x = jnp.concatenate([stage[b] for b in places], axis=1)
            o = lax.dot_general(
                x, whalo[side, k, :, : len(places) * LANES], (((1,), (1,)), ((), ())), preferred_element_type=F32
            )
            rest = gathered(o) * (inverse if is_first else twice)
            ybuf[j + 1, REACH + edges[side][k]] = partial[side, k] + rest

        put_stage(j, range(REACH, REACH + rows_here))
        for side in (0, 1):
            for k in range(REACH):
                if is_first:
                    prepare(edges[side][k])
                    prepare_halo(side, k)
                edge_own(side, k)
        if is_last:
            for r in inner:
                row(r)
            pl.semaphore_wait(relay.at[j], len(circle))
            send_packed(inner_peers)
        for side in (0, 1):
            halo_copy(j, 1 - side).wait_recv()
            put_stage(j, range(REACH + rows_here, 2 * REACH + rows_here) if side else range(REACH))
            for k in range(REACH):
                edge_rest(side, k)
            if is_last:
                send_packed(edge_peers[side])
            else:
                halo_copy(j + 1, side).start()

        if not is_last:
            for r in inner:
                if is_first:
                    prepare(r)
                row(r)
            pl.semaphore_wait(relay.at[j], len(circle))
            pass_word(j + 1)

        for side in (0, 1):
            halo_copy(j, side).wait_send()

    def later_step(j, carry):
        step(j, False, False)
        return carry

    step(0, True, False)
    lax.fori_loop(1, STEPS - 1, later_step, 0)
    step(STEPS - 1, False, True)
    arrived[w] = pack[w]

    half = z_size // 2

    def far_first(i):
        away = half - (i + 1) // 2
        return jnp.where(i % 2 == 0, z_size - away, away)

    def a2a_wait(k, carry):
        peer = (w + k) % wide
        a2a_copy(peer, peer).wait()
        return carry

    lax.fori_loop(1, wide, a2a_wait, 0)

    lane2 = lax.broadcasted_iota(jnp.int32, (HALVES * SUB, LANES), 1)

    for v in range(wide):
        tile = arrived[v]
        x = jnp.concatenate([tile, pltpu.roll(tile, LANES - share, 1)], axis=0)
        x = jnp.where(lane2 < share, x, 0.0)
        high, low = split_pair(x)
        rows = slice(v * HALVES * SUB, (v + 1) * HALVES * SUB)
        fmat[rows, :] = x
        amat[rows, 0:LANES] = (high + pltpu.roll(low, share, 1)).astype(BF16)
        amat[rows, LANES : 2 * LANES] = high.astype(BF16)
        bmat[rows, 0:LANES] = (high + pltpu.roll(high, share, 1)).astype(BF16)
        bmat[rows, LANES : 2 * LANES] = low.astype(BF16)

    side = fmat.shape[0] // LANES
    blocks_of = upper_blocks(side)
    for index, (i, j) in enumerate(blocks_of):
        gram[index * LANES : (index + 1) * LANES, :] = lax.dot_general(
            amat[i * LANES : (i + 1) * LANES, :],
            bmat[j * LANES : (j + 1) * LANES, :],
            (((1,), (1,)), ((), ())),
            preferred_element_type=F32,
        )

    chunk = gram.shape[0] // plane
    tiles = chunk // SUB
    stride = z_size // tiles

    def tile_rows(owner, t):
        return pl.ds(pl.multiple_of(owner * chunk + t * SUB, SUB), SUB)

    def owner_of(i):
        other = (z + far_first(i)) % z_size
        return other, (other % stride == 0) & (other < stride * tiles), jnp.minimum(other // stride, tiles - 1)

    def all_bytes(ref, sem):
        pltpu.make_async_copy(ref, ref, sem).wait()

    def plane_send(i, carry):
        _, owned, t = owner_of(i)

        @pl.when(owned)
        def _():
            for k, (peer, device) in enumerate(plane_peers):
                pltpu.make_async_remote_copy(
                    src_ref=gram.at[tile_rows(peer, t)],
                    dst_ref=plane_in.at[t, k],
                    send_sem=plane_sent.at[t],
                    recv_sem=plane_recv.at[t],
                    device_id=device,
                    device_id_type=MESH,
                ).start()

        return carry

    lax.fori_loop(0, z_size, plane_send, 0)

    def z_copy(other, t):
        return pltpu.make_async_remote_copy(
            src_ref=plane_sum.at[t],
            dst_ref=z_in.at[(other - z + z_size) % z_size - 1],
            send_sem=z_sent.at[t],
            recv_sem=z_recv,
            device_id=(n, y * z_size + other),
            device_id_type=MESH,
        )

    def bcast_copy(other, t):
        return pltpu.make_async_remote_copy(
            src_ref=z_sum,
            dst_ref=full.at[tile_rows(q, t)],
            send_sem=bcast_sent,
            recv_sem=bcast_recv.at[t],
            device_id=(n, y * z_size + other),
            device_id_type=MESH,
        )

    def plane_reduce(i, carry):
        other, owned, t = owner_of(i)

        @pl.when(owned)
        def _():
            all_bytes(plane_in.at[t], plane_recv.at[t])
            plane_sum[t] = gram[tile_rows(q, t), :] + jnp.sum(plane_in[t], axis=0)

        @pl.when(owned & (other != z))
        def _():
            z_copy(other, t).start()

        return carry

    lax.fori_loop(0, z_size, plane_reduce, 0)

    _, owner_here, mine = owner_of(z_size - 1)

    @pl.when(owner_here)
    def _():
        all_bytes(z_in, z_recv)
        z_sum[...] = plane_sum[mine] + jnp.sum(z_in[...], axis=0)

        def give(i, carry):
            bcast_copy((z + far_first(i)) % z_size, mine).start()
            return carry

        lax.fori_loop(0, z_size - 1, give, 0)
        full[tile_rows(q, mine), :] = z_sum[...]

    def gather_send(i, carry):
        other, owned, t = owner_of(z_size - 1 - i)

        @pl.when(owned & (other != z))
        def _():
            bcast_copy(z, t).wait_recv()

        @pl.when(owned)
        def _():
            for _, device in plane_peers:
                pltpu.make_async_remote_copy(
                    src_ref=full.at[tile_rows(q, t)],
                    dst_ref=full.at[tile_rows(q, t)],
                    send_sem=gather_sent.at[t],
                    recv_sem=gather_recv.at[t],
                    device_id=device,
                    device_id_type=MESH,
                ).start()

        return carry

    lax.fori_loop(0, z_size, gather_send, 0)

    for t in range(tiles):
        all_bytes(plane_in.at[t], gather_recv.at[t])

    squares = jnp.zeros((SUB, LANES), F32)
    for index, (i, j) in enumerate(blocks_of):
        block = full[index * LANES : (index + 1) * LANES, :]
        power = jnp.sum((block * block).reshape(LANES // SUB, SUB, LANES), axis=0)
        squares = squares + (power if i == j else 2.0 * power)
        high, low = split_pair(block)
        ghi[i * LANES : (i + 1) * LANES, j * LANES : (j + 1) * LANES] = high.astype(BF16)
        glo[i * LANES : (i + 1) * LANES, j * LANES : (j + 1) * LANES] = low.astype(BF16)
        if i != j:
            ghi[j * LANES : (j + 1) * LANES, i * LANES : (i + 1) * LANES] = high.T.astype(BF16)
            glo[j * LANES : (j + 1) * LANES, i * LANES : (i + 1) * LANES] = low.T.astype(BF16)

    frob = jnp.sqrt(jnp.sum(squares, keepdims=True) + 1e-06)
    scale = jnp.sqrt((total * LANES) / frob)
    main = 1.5 * scale
    cross = 0.5 * scale / frob
    fpair = amat[:, 0:LANES]
    for i in range(side):
        rows = slice(i * LANES, (i + 1) * LANES)
        zhi = jnp.dot(ghi[rows, :], fpair, preferred_element_type=F32)
        zlo = jnp.dot(glo[rows, :], fpair, preferred_element_type=F32)
        prod = (pltpu.roll(zhi, LANES - share, 1) + zlo) + zhi
        res = main * fmat[rows, :] - cross * prod
        out_ref[:, rows] = res.T[:share, :]

    for t in range(tiles):
        all_bytes(plane_in.at[t], plane_sent.at[t])
        all_bytes(plane_in.at[t], gather_sent.at[t])

    def z_drain(i, carry):
        other, owned, t = owner_of(i)

        @pl.when(owned & (other != z))
        def _():
            z_copy(other, t).wait_send()

        return carry

    lax.fori_loop(0, z_size, z_drain, 0)

    @pl.when(owner_here)
    def _():
        all_bytes(z_in, bcast_sent)


def on_device(cfg, vectors, blocks, columns, lower_bound, upper_bound):
    narrow, wide, z_size = cfg
    vecs, width = vectors.shape
    rows_here, slots = columns.shape
    count = vecs * wide
    side = count // LANES
    plane = narrow * (wide // z_size)
    gram_rows = len(upper_blocks(side)) * LANES
    tiles = gram_rows // plane // SUB
    ext = rows_here + 2 * REACH
    smem = pl.BlockSpec(memory_space=pltpu.SMEM)
    vmem = pl.BlockSpec(memory_space=pltpu.VMEM)
    hbm = pl.BlockSpec(memory_space=pltpu.HBM)
    dma = pltpu.SemaphoreType.DMA
    turned = pl.pallas_call(
        functools.partial(kernel_body, cfg),
        out_shape=jax.ShapeDtypeStruct((width // wide, count), F32),
        in_specs=[hbm, smem, smem, hbm, hbm],
        out_specs=vmem,
        scratch_shapes=[
            pltpu.VMEM((STEPS + 1, ext, vecs, LANES), F32),
            pltpu.VMEM((rows_here, 2 * LANES, slots * LANES), BF16),
            pltpu.VMEM((ext + 1, 2 * vecs, LANES), BF16),
            pltpu.VMEM((2, REACH, 2 * LANES, REACH * LANES), BF16),
            pltpu.VMEM((2, REACH, vecs, LANES), F32),
            pltpu.SMEM((rows_here, slots), jnp.int32),
            pltpu.SMEM((rows_here, slots), jnp.int32),
            pltpu.SMEM((slots, rows_here), jnp.int32),
            pltpu.VMEM((rows_here, slots, LANES, LANES), F32),
            pltpu.VMEM((wide, SUB, LANES), F32),
            pltpu.VMEM((wide, SUB, LANES), F32),
            pltpu.VMEM((count, LANES), F32),
            pltpu.VMEM((count, 2 * LANES), BF16),
            pltpu.VMEM((count, 2 * LANES), BF16),
            pltpu.VMEM((gram_rows, LANES), F32),
            pltpu.VMEM((tiles, plane - 1, SUB, LANES), F32),
            pltpu.VMEM((tiles, SUB, LANES), F32),
            pltpu.VMEM((z_size - 1, SUB, LANES), F32),
            pltpu.VMEM((SUB, LANES), F32),
            pltpu.VMEM((gram_rows, LANES), F32),
            pltpu.VMEM((count, count), BF16),
            pltpu.VMEM((count, count), BF16),
            dma((2,)),
            dma((rows_here,)),
            pltpu.SemaphoreType.REGULAR((STEPS,)),
            dma((STEPS, 2)),
            dma((STEPS, 2)),
            dma((wide,)),
            dma((wide,)),
            dma((tiles,)),
            dma((tiles,)),
            dma((tiles,)),
            dma,
            dma,
            dma((tiles,)),
            dma((tiles,)),
            dma((tiles,)),
        ],
        compiler_params=pltpu.CompilerParams(
            collective_id=0, has_side_effects=True, vmem_limit_bytes=67_043_328
        ),
    )(columns.T, lower_bound, upper_bound, vectors, blocks)
    return turned.T


def solution(mesh):
    cfg = (mesh.shape["narrow"], mesh.shape["wide"], Z_SIZE)
    return jax.shard_map(
        functools.partial(on_device, cfg),
        mesh=mesh,
        in_specs=(P("wide", "narrow"), P("narrow", None, None, None), P("narrow", None), P(), P()),
        out_specs=P(None, ("narrow", "wide")),
        check_vma=False,
    )
```

```python
import functools

import jax
import jax.numpy as jnp
from jax import lax
from jax.experimental import pallas as pl
from jax.experimental.pallas import tpu as pltpu
from jax.sharding import PartitionSpec as P

REACH = 3
STEPS = 8
LANES = 128
SUB = 8
HALVES = 2
Z_SIZE = 16
MESH = pl.DeviceIdType.MESH
F32 = jnp.float32
BF16 = jnp.bfloat16


def split_pair(value):
    high = value.astype(BF16).astype(F32)
    return high, value - high


def upper_blocks(count):
    return [(i, j) for i in range(count) for j in range(i, count)]


def kernel_body(
    cfg,
    cols_ref,
    low_ref,
    up_ref,
    vec_ref,
    blk_ref,
    out_ref,
    ybuf,
    wbuf,
    stage,
    whalo,
    partial,
    local_cols,
    own_cols,
    cols_in,
    blocks_in,
    pack,
    arrived,
    fmat,
    amat,
    bmat,
    gram,
    plane_in,
    plane_sum,
    z_in,
    z_sum,
    full,
    ghi,
    glo,
    load_sem,
    row_sem,
    relay,
    halo_send,
    halo_recv,
    send_sem,
    a2a_recv,
    plane_sent,
    plane_recv,
    z_sent,
    z_recv,
    bcast_sent,
    bcast_recv,
    gather_sent,
    gather_recv,
):
    narrow, wide, z_size = cfg
    slots, rows_here = cols_ref.shape
    vecs = vec_ref.shape[0]
    total = rows_here * narrow
    planes = wide // z_size
    plane = narrow * planes
    n = lax.axis_index("narrow")
    w = lax.axis_index("wide")
    z = w % z_size
    y = w // z_size
    q = y * narrow + n
    right, left = lax.rem(n + 1, narrow), lax.rem(n + narrow - 1, narrow)
    share = rows_here * LANES // wide

    planes = wide // z_size
    size_x, size_y = narrow // 4, planes * 2
    x, full_y, core = n // 4, y * 2 + lax.rem(n // 2, 2), lax.rem(n, 2)

    def hops(offset):
        return min(offset[0], size_x - offset[0]) + min(offset[1], size_y - offset[1])

    offsets = [(dx, dy, dc) for dx in range(size_x) for dy in range(size_y) for dc in range(2)][1:]
    plane_peers = []
    for dx, dy, dc in sorted(offsets, key=hops, reverse=True):
        peer_y = lax.rem(full_y + dy, size_y)
        peer_n = lax.rem(x + dx, size_x) * 4 + lax.rem(peer_y, 2) * 2 + lax.rem(core + dc, 2)
        plane_peers.append((peer_y // 2 * narrow + peer_n, (peer_n, peer_y // 2 * z_size + z)))

    def ring(dy, dz):
        return (n, ((y + dy) % (wide // z_size)) * z_size + (z + dz) % z_size)

    steps_y = {1: (), 2: (1,)}.get(wide // z_size, (1, wide // z_size - 1))
    circle = [(left, w), (right, w), ring(0, 1), ring(0, z_size - 1)] + [ring(dy, 0) for dy in steps_y]

    edges = [list(range(REACH)), list(range(rows_here - REACH, rows_here))]
    inner = list(range(REACH, rows_here - REACH))

    load_cols = pltpu.make_async_copy(cols_ref, cols_in, load_sem.at[0])
    load_cols.start()
    load_vec = [
        pltpu.make_async_copy(vec_ref.at[:, pl.ds(b * LANES, LANES)], ybuf.at[0, REACH + b], load_sem.at[1])
        for b in range(rows_here)
    ]
    for copy in load_vec:
        copy.start()
    load_rows = [pltpu.make_async_copy(blk_ref.at[r], blocks_in.at[r], row_sem.at[r]) for r in range(rows_here)]
    for r in edges[0] + edges[1] + inner:
        load_rows[r].start()

    barrier = pltpu.get_barrier_semaphore()
    for device in circle:
        pl.semaphore_signal(barrier, inc=1, device_id=device, device_id_type=MESH)

    whole = ybuf.at[0, pl.ds(REACH, rows_here)]
    pltpu.make_async_copy(whole, whole, load_sem.at[1]).wait()

    pl.semaphore_wait(barrier, len(circle))

    def pass_word(j):
        for device in circle:
            pl.semaphore_signal(relay.at[j], inc=1, device_id=device, device_id_type=MESH)

    def halo_copy(j, side):
        return pltpu.make_async_remote_copy(
            src_ref=ybuf.at[j, pl.ds(rows_here if side else REACH, REACH)],
            dst_ref=ybuf.at[j, pl.ds(0 if side else rows_here + REACH, REACH)],
            send_sem=halo_send.at[j, side],
            recv_sem=halo_recv.at[j, side],
            device_id=(right if side else left, w),
            device_id_type=MESH,
        )

    halo_copy(0, 0).start()
    halo_copy(0, 1).start()
    pass_word(0)

    load_cols.wait()
    first = n * rows_here
    for r in range(rows_here):
        for s in range(slots):
            at = cols_in[s, r] - first + REACH
            at = jnp.where(at < 0, at + total, at)
            at = jnp.where(at >= total, at - total, at)
            local_cols[r, s] = jnp.minimum(at, rows_here + 2 * REACH - 1)
            at_home = (at >= REACH) & (at < REACH + rows_here)
            own_cols[r, s] = jnp.where(at_home, at, rows_here + 2 * REACH)

    centre = jnp.full((vecs, LANES), (up_ref[0] + low_ref[0]) * 0.5, F32)
    inverse = 1.0 / jnp.full((vecs, LANES), (up_ref[0] - low_ref[0]) * 0.5, F32)
    keep = 1.0 - centre
    twice = 2.0 * inverse

    def paired(value):
        high, low = split_pair(value)
        return jnp.concatenate([high.astype(BF16), low.astype(BF16)], axis=0)

    def put_stage(j, blocks):
        for b in blocks:
            stage[b] = paired(ybuf[j, b])

    stage[rows_here + 2 * REACH] = jnp.zeros((2 * vecs, LANES), BF16)

    def halo_of(side, k):
        return range(rows_here + REACH, rows_here + REACH + k + 1) if side else range(k, REACH)

    def prepare(r):
        load_rows[r].wait()
        for s in range(slots):
            high, low = split_pair(blocks_in[r, s])
            wbuf[r, 0:LANES, s * LANES : (s + 1) * LANES] = high.astype(BF16)
            wbuf[r, LANES : 2 * LANES, s * LANES : (s + 1) * LANES] = low.astype(BF16)

    def prepare_halo(side, k):
        r = edges[side][k]
        for i, b in enumerate(halo_of(side, k)):
            total_block = jnp.zeros((LANES, LANES), F32)
            for s in range(slots):
                total_block = total_block + jnp.where(local_cols[r, s] == b, 1.0, 0.0).astype(F32) * blocks_in[r, s]
            high, low = split_pair(total_block)
            whalo[side, k, 0:LANES, i * LANES : (i + 1) * LANES] = high.astype(BF16)
            whalo[side, k, LANES : 2 * LANES, i * LANES : (i + 1) * LANES] = low.astype(BF16)

    lane = lax.broadcasted_iota(jnp.int32, (SUB, LANES), 1)

    def pack_one(peer):
        b0, off = divmod(peer * share, LANES)
        parts = []
        for h in range(HALVES):
            turn = (h * share - off) % LANES
            here = ybuf[STEPS, REACH + b0, h * SUB : (h + 1) * SUB, :]
            part = pltpu.roll(here, turn, 1) if turn else here
            if off + share > LANES:
                after = ybuf[STEPS, REACH + b0 + 1, h * SUB : (h + 1) * SUB, :]
                part2 = pltpu.roll(after, turn, 1) if turn else after
                part = jnp.where(lane < h * share + LANES - off, part, part2)
            parts.append(part)
        pack[peer] = jnp.where(lane < share, parts[0], parts[1])

    def a2a_copy(peer, slot):
        return pltpu.make_async_remote_copy(
            src_ref=pack.at[peer],
            dst_ref=arrived.at[slot],
            send_sem=send_sem.at[peer],
            recv_sem=a2a_recv.at[slot],
            device_id=(n, peer),
            device_id_type=MESH,
        )

    def send_packed(peers):
        for peer in peers:
            pack_one(peer)
        for peer in peers:

            @pl.when(w != peer)
            def _():
                a2a_copy(peer, w).start()

    def last_block(peer):
        return (peer * share + share - 1) // LANES

    edge_peers = [[p for p in range(wide) if p * share // LANES < REACH], []]
    inner_peers = [p for p in range(wide) if p * share // LANES >= REACH and last_block(p) < rows_here - REACH]
    edge_peers[1] = [p for p in range(wide) if p not in edge_peers[0] + inner_peers]
    assert all(last_block(p) < rows_here - REACH for p in edge_peers[0])

    def step(j, is_first, is_last):
        def gathered(o):
            return (o[:vecs, LANES:] + o[vecs:, :LANES]) + o[vecs:, LANES:] + o[:vecs, :LANES]

        def product(r):
            x = jnp.concatenate([stage[own_cols[r, s]] for s in range(slots)], axis=1)
            return gathered(lax.dot_general(x, wbuf[r], (((1,), (1,)), ((), ())), preferred_element_type=F32))

        def row(r):
            moved = keep * ybuf[j, REACH + r] + product(r)
            if is_first:
                ybuf[j + 1, REACH + r] = moved * inverse
            else:
                ybuf[j + 1, REACH + r] = moved * twice - ybuf[j - 1, REACH + r]

        def edge_own(side, k):
            r = edges[side][k]
            moved = keep * ybuf[j, REACH + r] + product(r)
            partial[side, k] = moved * inverse if is_first else moved * twice - ybuf[j - 1, REACH + r]

        def edge_rest(side, k, pieces):
            places = halo_of(side, k)
            x = jnp.concatenate([pieces[b] for b in places], axis=1)
            o = lax.dot_general(
                x, whalo[side, k, :, : len(places) * LANES], (((1,), (1,)), ((), ())), preferred_element_type=F32
            )
            rest = gathered(o) * (inverse if is_first else twice)
            ybuf[j + 1, REACH + edges[side][k]] = partial[side, k] + rest

        put_stage(j, range(REACH, REACH + rows_here))
        for side in (0, 1):
            for k in range(REACH):
                if is_first:
                    prepare(edges[side][k])
                    prepare_halo(side, k)
                edge_own(side, k)
        if is_last:
            for r in inner:
                row(r)
            pl.semaphore_wait(relay.at[j], len(circle))
            send_packed(inner_peers)
        for side in (0, 1):
            halo_copy(j, 1 - side).wait_recv()
            start = REACH + rows_here if side else 0
            pieces = {b: paired(ybuf[j, b]) for b in range(start, start + REACH)}
            for k in range(REACH):
                edge_rest(side, k, pieces)
            if is_last:
                send_packed(edge_peers[side])
            else:
                halo_copy(j + 1, side).start()

        if not is_last:
            for r in inner:
                if is_first:
                    prepare(r)
                row(r)
            pl.semaphore_wait(relay.at[j], len(circle))
            pass_word(j + 1)

        for side in (0, 1):
            halo_copy(j, side).wait_send()

    def later_step(j, carry):
        step(j, False, False)
        return carry

    step(0, True, False)
    lax.fori_loop(1, STEPS - 1, later_step, 0)
    step(STEPS - 1, False, True)
    arrived[w] = pack[w]

    def a2a_wait(k, carry):
        peer = (w + k) % wide
        a2a_copy(peer, peer).wait()
        return carry

    lax.fori_loop(1, wide, a2a_wait, 0)

    lane2 = lax.broadcasted_iota(jnp.int32, (HALVES * SUB, LANES), 1)

    for v in range(wide):
        tile = arrived[v]
        x = jnp.concatenate([tile, pltpu.roll(tile, LANES - share, 1)], axis=0)
        x = jnp.where(lane2 < share, x, 0.0)
        high, low = split_pair(x)
        rows = slice(v * HALVES * SUB, (v + 1) * HALVES * SUB)
        fmat[rows, :] = x
        amat[rows, 0:LANES] = (high + pltpu.roll(low, share, 1)).astype(BF16)
        amat[rows, LANES : 2 * LANES] = high.astype(BF16)
        bmat[rows, 0:LANES] = (high + pltpu.roll(high, share, 1)).astype(BF16)
        bmat[rows, LANES : 2 * LANES] = low.astype(BF16)

    side = fmat.shape[0] // LANES
    blocks_of = upper_blocks(side)
    for index, (i, j) in enumerate(blocks_of):
        gram[index * LANES : (index + 1) * LANES, :] = lax.dot_general(
            amat[i * LANES : (i + 1) * LANES, :],
            bmat[j * LANES : (j + 1) * LANES, :],
            (((1,), (1,)), ((), ())),
            preferred_element_type=F32,
        )

    chunk = gram.shape[0] // plane
    tiles = chunk // SUB
    half = z_size // 2
    assert tiles <= half == 8
    near = half // 2

    def tile_rows(owner, t):
        return pl.ds(pl.multiple_of(owner * chunk + t * SUB, SUB), SUB)

    def owner_of(i):
        up = jnp.where(i % 2 == 0, (z_size - (i + 1) // 2) % half, (i + 1) // 2)
        up = jnp.where(i == half - 1, near, up)
        t = (3 * ((z + up) % half)) % half
        return up, t < tiles, jnp.minimum(t, tiles - 1)

    def all_bytes(ref, sem):
        pltpu.make_async_copy(ref, ref, sem).wait()

    def plane_send(i, carry):
        _, owned, t = owner_of(i)

        @pl.when(owned)
        def _():
            for k, (peer, device) in enumerate(plane_peers):
                pltpu.make_async_remote_copy(
                    src_ref=gram.at[tile_rows(peer, t)],
                    dst_ref=plane_in.at[t, k],
                    send_sem=plane_sent.at[t],
                    recv_sem=plane_recv.at[t],
                    device_id=device,
                    device_id_type=MESH,
                ).start()

        return carry

    lax.fori_loop(0, half, plane_send, 0)

    def z_copy(up, t, second):
        there = (up + second * half) % z_size
        return pltpu.make_async_remote_copy(
            src_ref=plane_sum.at[t],
            dst_ref=z_in.at[(there + z_size - 1) % z_size],
            send_sem=z_sent.at[t, second],
            recv_sem=z_recv,
            device_id=(n, y * z_size + (z + there) % z_size),
            device_id_type=MESH,
        )

    def bcast_copy(down, t):
        return pltpu.make_async_remote_copy(
            src_ref=z_sum,
            dst_ref=full.at[tile_rows(q, t)],
            send_sem=bcast_sent,
            recv_sem=bcast_recv.at[t],
            device_id=(n, y * z_size + (z + z_size - down) % z_size),
            device_id_type=MESH,
        )

    def plane_reduce(i, carry):
        up, owned, t = owner_of(i)

        @pl.when(owned)
        def _():
            all_bytes(plane_in.at[t], plane_recv.at[t])
            plane_sum[t] = gram[tile_rows(q, t), :] + jnp.sum(plane_in[t], axis=0)
            z_copy(up, t, 1).start()

        @pl.when(owned & (up != 0))
        def _():
            z_copy(up, t, 0).start()

        return carry

    lax.fori_loop(0, half, plane_reduce, 0)

    _, owner_here, mine = owner_of(0)

    @pl.when(owner_here)
    def _():
        all_bytes(z_in, z_recv)
        z_sum[...] = plane_sum[mine] + jnp.sum(z_in[...], axis=0)
        for down in [near] + [d for k in range(near - 1, 0, -1) for d in (k, -k)]:
            bcast_copy(down, mine).start()
        full[tile_rows(q, mine), :] = z_sum[...]

    def gather_send(i, carry):
        up, owned, t = owner_of(i)

        @pl.when(owned & (up != 0))
        def _():
            bcast_copy(near, t).wait_recv()

        @pl.when(owned)
        def _():
            for _, device in plane_peers:
                pltpu.make_async_remote_copy(
                    src_ref=full.at[tile_rows(q, t)],
                    dst_ref=full.at[tile_rows(q, t)],
                    send_sem=gather_sent.at[t],
                    recv_sem=gather_recv.at[t],
                    device_id=device,
                    device_id_type=MESH,
                ).start()

        return carry

    lax.fori_loop(0, half, gather_send, 0)

    for t in range(tiles):
        all_bytes(plane_in.at[t], gather_recv.at[t])

    squares = jnp.zeros((SUB, LANES), F32)
    for index, (i, j) in enumerate(blocks_of):
        block = full[index * LANES : (index + 1) * LANES, :]
        power = jnp.sum((block * block).reshape(LANES // SUB, SUB, LANES), axis=0)
        squares = squares + (power if i == j else 2.0 * power)
        high, low = split_pair(block)
        ghi[i * LANES : (i + 1) * LANES, j * LANES : (j + 1) * LANES] = high.astype(BF16)
        glo[i * LANES : (i + 1) * LANES, j * LANES : (j + 1) * LANES] = low.astype(BF16)
        if i != j:
            ghi[j * LANES : (j + 1) * LANES, i * LANES : (i + 1) * LANES] = high.T.astype(BF16)
            glo[j * LANES : (j + 1) * LANES, i * LANES : (i + 1) * LANES] = low.T.astype(BF16)

    frob = jnp.sqrt(jnp.sum(squares, keepdims=True) + 1e-06)
    scale = jnp.sqrt((total * LANES) / frob)
    main = 1.5 * scale
    cross = 0.5 * scale / frob
    fpair = amat[:, 0:LANES]
    for i in range(side):
        rows = slice(i * LANES, (i + 1) * LANES)
        zhi = jnp.dot(ghi[rows, :], fpair, preferred_element_type=F32)
        zlo = jnp.dot(glo[rows, :], fpair, preferred_element_type=F32)
        prod = (pltpu.roll(zhi, LANES - share, 1) + zlo) + zhi
        res = main * fmat[rows, :] - cross * prod
        out_ref[:, rows] = res.T[:share, :]

    for t in range(tiles):
        all_bytes(plane_in.at[t], plane_sent.at[t])
        all_bytes(plane_in.at[t], gather_sent.at[t])

    def z_drain(i, carry):
        up, owned, t = owner_of(i)

        @pl.when(owned)
        def _():
            z_copy(up, t, 1).wait_send()

        @pl.when(owned & (up != 0))
        def _():
            z_copy(up, t, 0).wait_send()

        return carry

    lax.fori_loop(0, half, z_drain, 0)

    @pl.when(owner_here)
    def _():
        all_bytes(z_in.at[pl.ds(0, half - 1)], bcast_sent)


def on_device(cfg, vectors, blocks, columns, lower_bound, upper_bound):
    narrow, wide, z_size = cfg
    vecs, width = vectors.shape
    rows_here, slots = columns.shape
    count = vecs * wide
    side = count // LANES
    plane = narrow * (wide // z_size)
    gram_rows = len(upper_blocks(side)) * LANES
    tiles = gram_rows // plane // SUB
    ext = rows_here + 2 * REACH
    smem = pl.BlockSpec(memory_space=pltpu.SMEM)
    vmem = pl.BlockSpec(memory_space=pltpu.VMEM)
    hbm = pl.BlockSpec(memory_space=pltpu.HBM)
    dma = pltpu.SemaphoreType.DMA
    turned = pl.pallas_call(
        functools.partial(kernel_body, cfg),
        out_shape=jax.ShapeDtypeStruct((width // wide, count), F32),
        in_specs=[hbm, smem, smem, hbm, hbm],
        out_specs=vmem,
        scratch_shapes=[
            pltpu.VMEM((STEPS + 1, ext, vecs, LANES), F32),
            pltpu.VMEM((rows_here, 2 * LANES, slots * LANES), BF16),
            pltpu.VMEM((ext + 1, 2 * vecs, LANES), BF16),
            pltpu.VMEM((2, REACH, 2 * LANES, REACH * LANES), BF16),
            pltpu.VMEM((2, REACH, vecs, LANES), F32),
            pltpu.SMEM((rows_here, slots), jnp.int32),
            pltpu.SMEM((rows_here, slots), jnp.int32),
            pltpu.SMEM((slots, rows_here), jnp.int32),
            pltpu.VMEM((rows_here, slots, LANES, LANES), F32),
            pltpu.VMEM((wide, SUB, LANES), F32),
            pltpu.VMEM((wide, SUB, LANES), F32),
            pltpu.VMEM((count, LANES), F32),
            pltpu.VMEM((count, 2 * LANES), BF16),
            pltpu.VMEM((count, 2 * LANES), BF16),
            pltpu.VMEM((gram_rows, LANES), F32),
            pltpu.VMEM((tiles, plane - 1, SUB, LANES), F32),
            pltpu.VMEM((tiles, SUB, LANES), F32),
            pltpu.VMEM((z_size - 1, SUB, LANES), F32),
            pltpu.VMEM((SUB, LANES), F32),
            pltpu.VMEM((gram_rows, LANES), F32),
            pltpu.VMEM((count, count), BF16),
            pltpu.VMEM((count, count), BF16),
            dma((2,)),
            dma((rows_here,)),
            pltpu.SemaphoreType.REGULAR((STEPS,)),
            dma((STEPS, 2)),
            dma((STEPS, 2)),
            dma((wide,)),
            dma((wide,)),
            dma((tiles,)),
            dma((tiles,)),
            dma((tiles, 2)),
            dma,
            dma,
            dma((tiles,)),
            dma((tiles,)),
            dma((tiles,)),
        ],
        compiler_params=pltpu.CompilerParams(
            collective_id=0, has_side_effects=True, vmem_limit_bytes=67_043_328
        ),
    )(columns.T, lower_bound, upper_bound, vectors, blocks)
    return turned.T


def solution(mesh):
    cfg = (mesh.shape["narrow"], mesh.shape["wide"], Z_SIZE)
    return jax.shard_map(
        functools.partial(on_device, cfg),
        mesh=mesh,
        in_specs=(P("wide", "narrow"), P("narrow", None, None, None), P("narrow", None), P(), P()),
        out_specs=P(None, ("narrow", "wide")),
        check_vma=False,
    )
```

```python
import functools

import jax
import jax.numpy as jnp
from jax import lax
from jax.experimental import pallas as pl
from jax.experimental.pallas import tpu as pltpu
from jax.sharding import PartitionSpec as P

REACH = 3
STEPS = 8
LANES = 128
SUB = 8
HALVES = 2
Z_SIZE = 16
MESH = pl.DeviceIdType.MESH
F32 = jnp.float32
BF16 = jnp.bfloat16


def split_pair(value):
    high = value.astype(BF16).astype(F32)
    return high, value - high


def upper_blocks(count):
    return [(i, j) for i in range(count) for j in range(i, count)]


def kernel_body(
    cfg,
    cols_ref,
    low_ref,
    up_ref,
    vec_ref,
    blk_ref,
    out_ref,
    ybuf,
    wbuf,
    stage,
    whalo,
    partial,
    local_cols,
    own_cols,
    cols_in,
    blocks_in,
    pack,
    arrived,
    fmat,
    amat,
    bmat,
    gram,
    plane_in,
    plane_sum,
    z_in,
    z_sum,
    full,
    ghi,
    glo,
    load_sem,
    row_sem,
    relay,
    halo_send,
    halo_recv,
    send_sem,
    a2a_recv,
    plane_sent,
    plane_recv,
    z_sent,
    z_recv,
    bcast_sent,
    bcast_recv,
    gather_sent,
    gather_recv,
):
    narrow, wide, z_size = cfg
    slots, rows_here = cols_ref.shape
    vecs = vec_ref.shape[0]
    total = rows_here * narrow
    planes = wide // z_size
    plane = narrow * planes
    n = lax.axis_index("narrow")
    w = lax.axis_index("wide")
    z = w % z_size
    y = w // z_size
    q = y * narrow + n
    right, left = lax.rem(n + 1, narrow), lax.rem(n + narrow - 1, narrow)
    share = rows_here * LANES // wide

    planes = wide // z_size
    size_x, size_y = narrow // 4, planes * 2
    x, full_y, core = n // 4, y * 2 + lax.rem(n // 2, 2), lax.rem(n, 2)

    def hops(offset):
        return min(offset[0], size_x - offset[0]) + min(offset[1], size_y - offset[1])

    offsets = [(dx, dy, dc) for dx in range(size_x) for dy in range(size_y) for dc in range(2)][1:]
    plane_peers = []
    for dx, dy, dc in sorted(offsets, key=hops, reverse=True):
        peer_y = lax.rem(full_y + dy, size_y)
        peer_n = lax.rem(x + dx, size_x) * 4 + lax.rem(peer_y, 2) * 2 + lax.rem(core + dc, 2)
        plane_peers.append((peer_y // 2 * narrow + peer_n, (peer_n, peer_y // 2 * z_size + z)))

    def ring(dy, dz):
        return (n, ((y + dy) % (wide // z_size)) * z_size + (z + dz) % z_size)

    steps_y = {1: (), 2: (1,)}.get(wide // z_size, (1, wide // z_size - 1))
    circle = [(left, w), (right, w), ring(0, 1), ring(0, z_size - 1)] + [ring(dy, 0) for dy in steps_y]

    edges = [list(range(REACH)), list(range(rows_here - REACH, rows_here))]
    inner = list(range(REACH, rows_here - REACH))

    load_cols = pltpu.make_async_copy(cols_ref, cols_in, load_sem.at[0])
    load_cols.start()
    load_vec = [
        pltpu.make_async_copy(vec_ref.at[:, pl.ds(b * LANES, LANES)], ybuf.at[0, REACH + b], load_sem.at[1])
        for b in range(rows_here)
    ]
    for copy in load_vec:
        copy.start()
    load_rows = [pltpu.make_async_copy(blk_ref.at[r], blocks_in.at[r], row_sem.at[r]) for r in range(rows_here)]
    for r in edges[0] + edges[1] + inner:
        load_rows[r].start()

    barrier = pltpu.get_barrier_semaphore()
    for device in circle:
        pl.semaphore_signal(barrier, inc=1, device_id=device, device_id_type=MESH)

    whole = ybuf.at[0, pl.ds(REACH, rows_here)]
    pltpu.make_async_copy(whole, whole, load_sem.at[1]).wait()

    pl.semaphore_wait(barrier, len(circle))

    def pass_word(j):
        for device in circle:
            pl.semaphore_signal(relay.at[j], inc=1, device_id=device, device_id_type=MESH)

    def halo_copy(j, side, k):
        return pltpu.make_async_remote_copy(
            src_ref=ybuf.at[j, (rows_here if side else REACH) + k],
            dst_ref=ybuf.at[j, (0 if side else rows_here + REACH) + k],
            send_sem=halo_send.at[j, side, k],
            recv_sem=halo_recv.at[j, side, k],
            device_id=(right if side else left, w),
            device_id_type=MESH,
        )

    def deepest_first(side):
        return range(REACH - 1, -1, -1) if side else range(REACH)

    for side in (0, 1):
        for k in range(REACH):
            halo_copy(0, side, k).start()
    pass_word(0)

    load_cols.wait()
    first = n * rows_here
    for r in range(rows_here):
        for s in range(slots):
            at = cols_in[s, r] - first + REACH
            at = jnp.where(at < 0, at + total, at)
            at = jnp.where(at >= total, at - total, at)
            local_cols[r, s] = jnp.minimum(at, rows_here + 2 * REACH - 1)
            at_home = (at >= REACH) & (at < REACH + rows_here)
            own_cols[r, s] = jnp.where(at_home, at, rows_here + 2 * REACH)

    centre = jnp.full((vecs, LANES), (up_ref[0] + low_ref[0]) * 0.5, F32)
    inverse = 1.0 / jnp.full((vecs, LANES), (up_ref[0] - low_ref[0]) * 0.5, F32)
    keep = 1.0 - centre
    twice = 2.0 * inverse

    def paired(value):
        high, low = split_pair(value)
        return jnp.concatenate([high.astype(BF16), low.astype(BF16)], axis=0)

    def put_stage(j, blocks):
        for b in blocks:
            stage[b] = paired(ybuf[j, b])

    stage[rows_here + 2 * REACH] = jnp.zeros((2 * vecs, LANES), BF16)

    def halo_of(side, k):
        return range(rows_here + REACH, rows_here + REACH + k + 1) if side else range(k, REACH)

    def prepare(r):
        load_rows[r].wait()
        for s in range(slots):
            high, low = split_pair(blocks_in[r, s])
            wbuf[r, 0:LANES, s * LANES : (s + 1) * LANES] = high.astype(BF16)
            wbuf[r, LANES : 2 * LANES, s * LANES : (s + 1) * LANES] = low.astype(BF16)

    def prepare_halo(side, k):
        r = edges[side][k]
        for i, b in enumerate(halo_of(side, k)):
            total_block = jnp.zeros((LANES, LANES), F32)
            for s in range(slots):
                total_block = total_block + jnp.where(local_cols[r, s] == b, 1.0, 0.0).astype(F32) * blocks_in[r, s]
            high, low = split_pair(total_block)
            whalo[side, k, 0:LANES, i * LANES : (i + 1) * LANES] = high.astype(BF16)
            whalo[side, k, LANES : 2 * LANES, i * LANES : (i + 1) * LANES] = low.astype(BF16)

    lane = lax.broadcasted_iota(jnp.int32, (SUB, LANES), 1)

    def pack_one(peer):
        b0, off = divmod(peer * share, LANES)
        parts = []
        for h in range(HALVES):
            turn = (h * share - off) % LANES
            here = ybuf[STEPS, REACH + b0, h * SUB : (h + 1) * SUB, :]
            part = pltpu.roll(here, turn, 1) if turn else here
            if off + share > LANES:
                after = ybuf[STEPS, REACH + b0 + 1, h * SUB : (h + 1) * SUB, :]
                part2 = pltpu.roll(after, turn, 1) if turn else after
                part = jnp.where(lane < h * share + LANES - off, part, part2)
            parts.append(part)
        pack[peer] = jnp.where(lane < share, parts[0], parts[1])

    def a2a_copy(peer, slot):
        return pltpu.make_async_remote_copy(
            src_ref=pack.at[peer],
            dst_ref=arrived.at[slot],
            send_sem=send_sem.at[peer],
            recv_sem=a2a_recv.at[slot],
            device_id=(n, peer),
            device_id_type=MESH,
        )

    def send_packed(peers):
        for peer in peers:
            pack_one(peer)
        for peer in peers:

            @pl.when(w != peer)
            def _():
                a2a_copy(peer, w).start()

    def last_block(peer):
        return (peer * share + share - 1) // LANES

    edge_peers = [[p for p in range(wide) if p * share // LANES < REACH], []]
    inner_peers = [p for p in range(wide) if p * share // LANES >= REACH and last_block(p) < rows_here - REACH]
    edge_peers[1] = [p for p in range(wide) if p not in edge_peers[0] + inner_peers]
    assert all(last_block(p) < rows_here - REACH for p in edge_peers[0])

    def step(j, is_first, is_last):
        def gathered(o):
            return (o[:vecs, LANES:] + o[vecs:, :LANES]) + o[vecs:, LANES:] + o[:vecs, :LANES]

        def product(r):
            x = jnp.concatenate([stage[own_cols[r, s]] for s in range(slots)], axis=1)
            return gathered(lax.dot_general(x, wbuf[r], (((1,), (1,)), ((), ())), preferred_element_type=F32))

        def row(r):
            moved = keep * ybuf[j, REACH + r] + product(r)
            if is_first:
                ybuf[j + 1, REACH + r] = moved * inverse
            else:
                ybuf[j + 1, REACH + r] = moved * twice - ybuf[j - 1, REACH + r]

        def edge_own(side, k):
            r = edges[side][k]
            moved = keep * ybuf[j, REACH + r] + product(r)
            partial[side, k] = moved * inverse if is_first else moved * twice - ybuf[j - 1, REACH + r]

        def edge_rest(side, k, pieces):
            places = halo_of(side, k)
            x = jnp.concatenate([pieces[b] for b in places], axis=1)
            o = lax.dot_general(
                x, whalo[side, k, :, : len(places) * LANES], (((1,), (1,)), ((), ())), preferred_element_type=F32
            )
            rest = gathered(o) * (inverse if is_first else twice)
            ybuf[j + 1, REACH + edges[side][k]] = partial[side, k] + rest

        put_stage(j, range(REACH, REACH + rows_here))
        for side in (0, 1):
            for k in range(REACH):
                if is_first:
                    prepare(edges[side][k])
                    prepare_halo(side, k)
                edge_own(side, k)
        if is_last:
            for r in inner:
                row(r)
            pl.semaphore_wait(relay.at[j], len(circle))
            send_packed(inner_peers)
        for side in (0, 1):
            for k in range(REACH):
                halo_copy(j, 1 - side, k).wait_recv()
            start = REACH + rows_here if side else 0
            pieces = {b: paired(ybuf[j, b]) for b in range(start, start + REACH)}
            for k in deepest_first(side):
                edge_rest(side, k, pieces)
                if not is_last:
                    halo_copy(j + 1, side, k).start()
            if is_last:
                send_packed(edge_peers[side])

        if not is_last:
            for r in inner:
                if is_first:
                    prepare(r)
                row(r)
            pl.semaphore_wait(relay.at[j], len(circle))
            pass_word(j + 1)

        for side in (0, 1):
            for k in range(REACH):
                halo_copy(j, side, k).wait_send()

    def later_step(j, carry):
        step(j, False, False)
        return carry

    step(0, True, False)
    lax.fori_loop(1, STEPS - 1, later_step, 0)
    step(STEPS - 1, False, True)
    arrived[w] = pack[w]

    lane2 = lax.broadcasted_iota(jnp.int32, (HALVES * SUB, LANES), 1)

    def wide_hops(offset):
        return 2 * min(offset[0], planes - offset[0]) + min(offset[1], z_size - offset[1])

    senders = []
    for dy, dz in sorted([(dy, dz) for dy in range(planes) for dz in range(z_size)], key=wide_hops):
        senders.append(lax.rem(y + dy, planes) * z_size + lax.rem(z + dz, z_size))
    for count, v in enumerate(senders):
        if count % 8 == 0:
            for sender in senders[max(count, 1) : count + 8]:
                a2a_copy(sender, sender).wait()
        tile = arrived[v]
        x = jnp.concatenate([tile, pltpu.roll(tile, LANES - share, 1)], axis=0)
        x = jnp.where(lane2 < share, x, 0.0)
        high, low = split_pair(x)
        rows = pl.ds(pl.multiple_of(v * HALVES * SUB, HALVES * SUB), HALVES * SUB)
        fmat[rows, :] = x
        amat[rows, 0:LANES] = (high + pltpu.roll(low, share, 1)).astype(BF16)
        amat[rows, LANES : 2 * LANES] = high.astype(BF16)
        bmat[rows, 0:LANES] = (high + pltpu.roll(high, share, 1)).astype(BF16)
        bmat[rows, LANES : 2 * LANES] = low.astype(BF16)

    side = fmat.shape[0] // LANES
    blocks_of = upper_blocks(side)
    for index, (i, j) in enumerate(blocks_of):
        gram[index * LANES : (index + 1) * LANES, :] = lax.dot_general(
            amat[i * LANES : (i + 1) * LANES, :],
            bmat[j * LANES : (j + 1) * LANES, :],
            (((1,), (1,)), ((), ())),
            preferred_element_type=F32,
        )

    chunk = gram.shape[0] // plane
    tiles = chunk // SUB
    half = z_size // 2
    assert tiles <= half == 8
    near = half // 2

    def tile_rows(owner, t):
        return pl.ds(pl.multiple_of(owner * chunk + t * SUB, SUB), SUB)

    def owner_of(i):
        up = jnp.where(i % 2 == 0, (z_size - (i + 1) // 2) % half, (i + 1) // 2)
        up = jnp.where(i == half - 1, near, up)
        t = (3 * ((z + up) % half)) % half
        return up, t < tiles, jnp.minimum(t, tiles - 1)

    def all_bytes(ref, sem):
        pltpu.make_async_copy(ref, ref, sem).wait()

    def plane_send(i, carry):
        _, owned, t = owner_of(i)

        @pl.when(owned)
        def _():
            for k, (peer, device) in enumerate(plane_peers):
                pltpu.make_async_remote_copy(
                    src_ref=gram.at[tile_rows(peer, t)],
                    dst_ref=plane_in.at[t, k],
                    send_sem=plane_sent.at[t],
                    recv_sem=plane_recv.at[t],
                    device_id=device,
                    device_id_type=MESH,
                ).start()

        return carry

    lax.fori_loop(0, half, plane_send, 0)

    def z_copy(up, t, second):
        there = (up + second * half) % z_size
        return pltpu.make_async_remote_copy(
            src_ref=plane_sum.at[t],
            dst_ref=z_in.at[(there + z_size - 1) % z_size],
            send_sem=z_sent.at[t, second],
            recv_sem=z_recv,
            device_id=(n, y * z_size + (z + there) % z_size),
            device_id_type=MESH,
        )

    def bcast_copy(down, t):
        return pltpu.make_async_remote_copy(
            src_ref=z_sum,
            dst_ref=full.at[tile_rows(q, t)],
            send_sem=bcast_sent,
            recv_sem=bcast_recv.at[t],
            device_id=(n, y * z_size + (z + z_size - down) % z_size),
            device_id_type=MESH,
        )

    def plane_reduce(i, carry):
        up, owned, t = owner_of(i)

        @pl.when(owned)
        def _():
            all_bytes(plane_in.at[t], plane_recv.at[t])
            plane_sum[t] = gram[tile_rows(q, t), :] + jnp.sum(plane_in[t], axis=0)
            z_copy(up, t, 1).start()

        @pl.when(owned & (up != 0))
        def _():
            z_copy(up, t, 0).start()

        return carry

    lax.fori_loop(0, half, plane_reduce, 0)

    _, owner_here, mine = owner_of(0)

    @pl.when(owner_here)
    def _():
        all_bytes(z_in, z_recv)
        z_sum[...] = plane_sum[mine] + jnp.sum(z_in[...], axis=0)
        for down in [near] + [d for k in range(near - 1, 0, -1) for d in (k, -k)]:
            bcast_copy(down, mine).start()
        full[tile_rows(q, mine), :] = z_sum[...]

    def gather_send(i, carry):
        up, owned, t = owner_of(i)

        @pl.when(owned & (up != 0))
        def _():
            bcast_copy(near, t).wait_recv()

        @pl.when(owned)
        def _():
            for _, device in plane_peers:
                pltpu.make_async_remote_copy(
                    src_ref=full.at[tile_rows(q, t)],
                    dst_ref=full.at[tile_rows(q, t)],
                    send_sem=gather_sent.at[t],
                    recv_sem=gather_recv.at[t],
                    device_id=device,
                    device_id_type=MESH,
                ).start()

        return carry

    lax.fori_loop(0, half, gather_send, 0)

    for t in range(tiles):
        all_bytes(plane_in.at[t], gather_recv.at[t])

    squares = jnp.zeros((SUB, LANES), F32)
    for index, (i, j) in enumerate(blocks_of):
        block = full[index * LANES : (index + 1) * LANES, :]
        power = jnp.sum((block * block).reshape(LANES // SUB, SUB, LANES), axis=0)
        squares = squares + (power if i == j else 2.0 * power)
        high, low = split_pair(block)
        ghi[i * LANES : (i + 1) * LANES, j * LANES : (j + 1) * LANES] = high.astype(BF16)
        glo[i * LANES : (i + 1) * LANES, j * LANES : (j + 1) * LANES] = low.astype(BF16)
        if i != j:
            ghi[j * LANES : (j + 1) * LANES, i * LANES : (i + 1) * LANES] = high.T.astype(BF16)
            glo[j * LANES : (j + 1) * LANES, i * LANES : (i + 1) * LANES] = low.T.astype(BF16)

    frob = jnp.sqrt(jnp.sum(squares, keepdims=True) + 1e-06)
    scale = jnp.sqrt((total * LANES) / frob)
    main = 1.5 * scale
    cross = 0.5 * scale / frob
    fpair = amat[:, 0:LANES]
    for i in range(side):
        rows = slice(i * LANES, (i + 1) * LANES)
        zhi = jnp.dot(ghi[rows, :], fpair, preferred_element_type=F32)
        zlo = jnp.dot(glo[rows, :], fpair, preferred_element_type=F32)
        prod = (pltpu.roll(zhi, LANES - share, 1) + zlo) + zhi
        res = main * fmat[rows, :] - cross * prod
        out_ref[:, rows] = res.T[:share, :]

    for t in range(tiles):
        all_bytes(plane_in.at[t], plane_sent.at[t])
        all_bytes(plane_in.at[t], gather_sent.at[t])

    def z_drain(i, carry):
        up, owned, t = owner_of(i)

        @pl.when(owned)
        def _():
            z_copy(up, t, 1).wait_send()

        @pl.when(owned & (up != 0))
        def _():
            z_copy(up, t, 0).wait_send()

        return carry

    lax.fori_loop(0, half, z_drain, 0)

    @pl.when(owner_here)
    def _():
        all_bytes(z_in.at[pl.ds(0, half - 1)], bcast_sent)


def on_device(cfg, vectors, blocks, columns, lower_bound, upper_bound):
    narrow, wide, z_size = cfg
    vecs, width = vectors.shape
    rows_here, slots = columns.shape
    count = vecs * wide
    side = count // LANES
    plane = narrow * (wide // z_size)
    gram_rows = len(upper_blocks(side)) * LANES
    tiles = gram_rows // plane // SUB
    ext = rows_here + 2 * REACH
    smem = pl.BlockSpec(memory_space=pltpu.SMEM)
    vmem = pl.BlockSpec(memory_space=pltpu.VMEM)
    hbm = pl.BlockSpec(memory_space=pltpu.HBM)
    dma = pltpu.SemaphoreType.DMA
    turned = pl.pallas_call(
        functools.partial(kernel_body, cfg),
        out_shape=jax.ShapeDtypeStruct((width // wide, count), F32),
        in_specs=[hbm, smem, smem, hbm, hbm],
        out_specs=vmem,
        scratch_shapes=[
            pltpu.VMEM((STEPS + 1, ext, vecs, LANES), F32),
            pltpu.VMEM((rows_here, 2 * LANES, slots * LANES), BF16),
            pltpu.VMEM((ext + 1, 2 * vecs, LANES), BF16),
            pltpu.VMEM((2, REACH, 2 * LANES, REACH * LANES), BF16),
            pltpu.VMEM((2, REACH, vecs, LANES), F32),
            pltpu.SMEM((rows_here, slots), jnp.int32),
            pltpu.SMEM((rows_here, slots), jnp.int32),
            pltpu.SMEM((slots, rows_here), jnp.int32),
            pltpu.VMEM((rows_here, slots, LANES, LANES), F32),
            pltpu.VMEM((wide, SUB, LANES), F32),
            pltpu.VMEM((wide, SUB, LANES), F32),
            pltpu.VMEM((count, LANES), F32),
            pltpu.VMEM((count, 2 * LANES), BF16),
            pltpu.VMEM((count, 2 * LANES), BF16),
            pltpu.VMEM((gram_rows, LANES), F32),
            pltpu.VMEM((tiles, plane - 1, SUB, LANES), F32),
            pltpu.VMEM((tiles, SUB, LANES), F32),
            pltpu.VMEM((z_size - 1, SUB, LANES), F32),
            pltpu.VMEM((SUB, LANES), F32),
            pltpu.VMEM((gram_rows, LANES), F32),
            pltpu.VMEM((count, count), BF16),
            pltpu.VMEM((count, count), BF16),
            dma((2,)),
            dma((rows_here,)),
            pltpu.SemaphoreType.REGULAR((STEPS,)),
            dma((STEPS, 2, REACH)),
            dma((STEPS, 2, REACH)),
            dma((wide,)),
            dma((wide,)),
            dma((tiles,)),
            dma((tiles,)),
            dma((tiles, 2)),
            dma,
            dma,
            dma((tiles,)),
            dma((tiles,)),
            dma((tiles,)),
        ],
        compiler_params=pltpu.CompilerParams(
            collective_id=0, has_side_effects=True, vmem_limit_bytes=67_043_328
        ),
    )(columns.T, lower_bound, upper_bound, vectors, blocks)
    return turned.T


def solution(mesh):
    cfg = (mesh.shape["narrow"], mesh.shape["wide"], Z_SIZE)
    return jax.shard_map(
        functools.partial(on_device, cfg),
        mesh=mesh,
        in_specs=(P("wide", "narrow"), P("narrow", None, None, None), P("narrow", None), P(), P()),
        out_specs=P(None, ("narrow", "wide")),
        check_vma=False,
    )
```

```python
import functools

import jax
import jax.numpy as jnp
from jax import lax
from jax.experimental import pallas as pl
from jax.experimental.pallas import tpu as pltpu
from jax.sharding import PartitionSpec as P

REACH = 3
STEPS = 8
LANES = 128
SUB = 8
HALVES = 2
Z_SIZE = 16
MESH = pl.DeviceIdType.MESH
F32 = jnp.float32
BF16 = jnp.bfloat16


def split_pair(value):
    high = value.astype(BF16).astype(F32)
    return high, value - high


def upper_blocks(count):
    return [(i, j) for i in range(count) for j in range(i, count)]


def kernel_body(
    cfg,
    cols_ref,
    low_ref,
    up_ref,
    vec_ref,
    blk_ref,
    out_ref,
    ybuf,
    wbuf,
    stage,
    whalo,
    partial,
    local_cols,
    own_cols,
    cols_in,
    blocks_in,
    pack,
    arrived,
    fmat,
    amat,
    bmat,
    gram,
    core_in,
    core_sum,
    plane_in,
    plane_sum,
    z_in,
    z_sum,
    full,
    ghi,
    glo,
    load_sem,
    row_sem,
    relay,
    halo_send,
    halo_recv,
    send_sem,
    a2a_recv,
    core_sent,
    core_recv,
    hand_sent,
    hand_recv,
    plane_sent,
    plane_recv,
    z_sent,
    z_recv,
    bcast_sent,
    bcast_recv,
    gather_sent,
    gather_recv,
):
    narrow, wide, z_size = cfg
    slots, rows_here = cols_ref.shape
    vecs = vec_ref.shape[0]
    total = rows_here * narrow
    planes = wide // z_size
    plane = narrow * planes
    n = lax.axis_index("narrow")
    w = lax.axis_index("wide")
    z = w % z_size
    y = w // z_size
    q = y * narrow + n
    right, left = lax.rem(n + 1, narrow), lax.rem(n + narrow - 1, narrow)
    share = rows_here * LANES // wide

    planes = wide // z_size
    size_x, size_y = narrow // 4, planes * 2
    x, full_y, core = n // 4, y * 2 + lax.rem(n // 2, 2), lax.rem(n, 2)

    def hops(offset):
        return min(offset[0], size_x - offset[0]) + min(offset[1], size_y - offset[1])

    offsets = [(dx, dy, dc) for dx in range(size_x) for dy in range(size_y) for dc in range(2)][1:]
    plane_peers, core_peers = [], []
    for dx, dy, dc in sorted(offsets, key=hops, reverse=True):
        peer_y = lax.rem(full_y + dy, size_y)
        peer_n = lax.rem(x + dx, size_x) * 4 + lax.rem(peer_y, 2) * 2 + lax.rem(core + dc, 2)
        plane_peers.append((peer_y // 2 * narrow + peer_n, (peer_n, peer_y // 2 * z_size + z)))
        if dc == 0:
            core_peers.append(plane_peers[-1])

    def ring(dy, dz):
        return (n, ((y + dy) % (wide // z_size)) * z_size + (z + dz) % z_size)

    steps_y = {1: (), 2: (1,)}.get(wide // z_size, (1, wide // z_size - 1))
    circle = [(left, w), (right, w), ring(0, 1), ring(0, z_size - 1)] + [ring(dy, 0) for dy in steps_y]

    edges = [list(range(REACH)), list(range(rows_here - REACH, rows_here))]
    inner = list(range(REACH, rows_here - REACH))

    load_cols = pltpu.make_async_copy(cols_ref, cols_in, load_sem.at[0])
    load_cols.start()
    load_vec = [
        pltpu.make_async_copy(vec_ref.at[:, pl.ds(b * LANES, LANES)], ybuf.at[0, REACH + b], load_sem.at[1])
        for b in range(rows_here)
    ]
    for copy in load_vec:
        copy.start()
    load_rows = [pltpu.make_async_copy(blk_ref.at[r], blocks_in.at[r], row_sem.at[r]) for r in range(rows_here)]
    for r in edges[0] + edges[1] + inner:
        load_rows[r].start()

    barrier = pltpu.get_barrier_semaphore()
    for device in circle:
        pl.semaphore_signal(barrier, inc=1, device_id=device, device_id_type=MESH)

    whole = ybuf.at[0, pl.ds(REACH, rows_here)]
    pltpu.make_async_copy(whole, whole, load_sem.at[1]).wait()

    pl.semaphore_wait(barrier, len(circle))

    def pass_word(j):
        for device in circle:
            pl.semaphore_signal(relay.at[j], inc=1, device_id=device, device_id_type=MESH)

    def halo_copy(j, side):
        return pltpu.make_async_remote_copy(
            src_ref=ybuf.at[j, pl.ds(rows_here if side else REACH, REACH)],
            dst_ref=ybuf.at[j, pl.ds(0 if side else rows_here + REACH, REACH)],
            send_sem=halo_send.at[j, side],
            recv_sem=halo_recv.at[j, side],
            device_id=(right if side else left, w),
            device_id_type=MESH,
        )

    halo_copy(0, 0).start()
    halo_copy(0, 1).start()
    pass_word(0)

    load_cols.wait()
    first = n * rows_here
    for r in range(rows_here):
        for s in range(slots):
            at = cols_in[s, r] - first + REACH
            at = jnp.where(at < 0, at + total, at)
            at = jnp.where(at >= total, at - total, at)
            local_cols[r, s] = jnp.minimum(at, rows_here + 2 * REACH - 1)
            at_home = (at >= REACH) & (at < REACH + rows_here)
            own_cols[r, s] = jnp.where(at_home, at, rows_here + 2 * REACH)

    centre = jnp.full((vecs, LANES), (up_ref[0] + low_ref[0]) * 0.5, F32)
    inverse = 1.0 / jnp.full((vecs, LANES), (up_ref[0] - low_ref[0]) * 0.5, F32)
    keep = 1.0 - centre
    twice = 2.0 * inverse

    def paired(value):
        high, low = split_pair(value)
        return jnp.concatenate([high.astype(BF16), low.astype(BF16)], axis=0)

    def put_stage(j, blocks):
        for b in blocks:
            stage[b] = paired(ybuf[j, b])

    stage[rows_here + 2 * REACH] = jnp.zeros((2 * vecs, LANES), BF16)

    def halo_of(side, k):
        return range(rows_here + REACH, rows_here + REACH + k + 1) if side else range(k, REACH)

    def prepare(r):
        load_rows[r].wait()
        for s in range(slots):
            high, low = split_pair(blocks_in[r, s])
            wbuf[r, 0:LANES, s * LANES : (s + 1) * LANES] = high.astype(BF16)
            wbuf[r, LANES : 2 * LANES, s * LANES : (s + 1) * LANES] = low.astype(BF16)

    def prepare_halo(side, k):
        r = edges[side][k]
        for i, b in enumerate(halo_of(side, k)):
            total_block = jnp.zeros((LANES, LANES), F32)
            for s in range(slots):
                total_block = total_block + jnp.where(local_cols[r, s] == b, 1.0, 0.0).astype(F32) * blocks_in[r, s]
            high, low = split_pair(total_block)
            whalo[side, k, 0:LANES, i * LANES : (i + 1) * LANES] = high.astype(BF16)
            whalo[side, k, LANES : 2 * LANES, i * LANES : (i + 1) * LANES] = low.astype(BF16)

    lane = lax.broadcasted_iota(jnp.int32, (SUB, LANES), 1)

    def pack_one(peer):
        b0, off = divmod(peer * share, LANES)
        parts = []
        for h in range(HALVES):
            turn = (h * share - off) % LANES
            here = ybuf[STEPS, REACH + b0, h * SUB : (h + 1) * SUB, :]
            part = pltpu.roll(here, turn, 1) if turn else here
            if off + share > LANES:
                after = ybuf[STEPS, REACH + b0 + 1, h * SUB : (h + 1) * SUB, :]
                part2 = pltpu.roll(after, turn, 1) if turn else after
                part = jnp.where(lane < h * share + LANES - off, part, part2)
            parts.append(part)
        pack[peer] = jnp.where(lane < share, parts[0], parts[1])

    def a2a_copy(peer, slot):
        return pltpu.make_async_remote_copy(
            src_ref=pack.at[peer],
            dst_ref=arrived.at[slot],
            send_sem=send_sem.at[peer],
            recv_sem=a2a_recv.at[slot],
            device_id=(n, peer),
            device_id_type=MESH,
        )

    def send_packed(peers):
        for peer in peers:
            pack_one(peer)
        for peer in peers:

            @pl.when(w != peer)
            def _():
                a2a_copy(peer, w).start()

    def last_block(peer):
        return (peer * share + share - 1) // LANES

    edge_peers = [[p for p in range(wide) if p * share // LANES < REACH], []]
    inner_peers = [p for p in range(wide) if p * share // LANES >= REACH and last_block(p) < rows_here - REACH]
    edge_peers[1] = [p for p in range(wide) if p not in edge_peers[0] + inner_peers]
    assert all(last_block(p) < rows_here - REACH for p in edge_peers[0])

    def step(j, is_first, is_last):
        def gathered(o):
            return (o[:vecs, LANES:] + o[vecs:, :LANES]) + o[vecs:, LANES:] + o[:vecs, :LANES]

        def product(r):
            x = jnp.concatenate([stage[own_cols[r, s]] for s in range(slots)], axis=1)
            return gathered(lax.dot_general(x, wbuf[r], (((1,), (1,)), ((), ())), preferred_element_type=F32))

        def row(r):
            moved = keep * ybuf[j, REACH + r] + product(r)
            if is_first:
                ybuf[j + 1, REACH + r] = moved * inverse
            else:
                ybuf[j + 1, REACH + r] = moved * twice - ybuf[j - 1, REACH + r]

        def edge_own(side, k):
            r = edges[side][k]
            moved = keep * ybuf[j, REACH + r] + product(r)
            partial[side, k] = moved * inverse if is_first else moved * twice - ybuf[j - 1, REACH + r]

        def edge_rest(side, k, pieces):
            places = halo_of(side, k)
            x = jnp.concatenate([pieces[b] for b in places], axis=1)
            o = lax.dot_general(
                x, whalo[side, k, :, : len(places) * LANES], (((1,), (1,)), ((), ())), preferred_element_type=F32
            )
            rest = gathered(o) * (inverse if is_first else twice)
            ybuf[j + 1, REACH + edges[side][k]] = partial[side, k] + rest

        put_stage(j, range(REACH, REACH + rows_here))
        for side in (0, 1):
            for k in range(REACH):
                if is_first:
                    prepare(edges[side][k])
                    prepare_halo(side, k)
                edge_own(side, k)
        if is_last:
            for r in inner:
                row(r)
            pl.semaphore_wait(relay.at[j], len(circle))
            send_packed(inner_peers)
        for side in (0, 1):
            halo_copy(j, 1 - side).wait_recv()
            start = REACH + rows_here if side else 0
            pieces = {b: paired(ybuf[j, b]) for b in range(start, start + REACH)}
            for k in range(REACH):
                edge_rest(side, k, pieces)
            if is_last:
                send_packed(edge_peers[side])
            else:
                halo_copy(j + 1, side).start()

        if not is_last:
            for r in inner:
                if is_first:
                    prepare(r)
                row(r)
            pl.semaphore_wait(relay.at[j], len(circle))
            pass_word(j + 1)

        for side in (0, 1):
            halo_copy(j, side).wait_send()

    def later_step(j, carry):
        step(j, False, False)
        return carry

    step(0, True, False)
    lax.fori_loop(1, STEPS - 1, later_step, 0)
    step(STEPS - 1, False, True)
    arrived[w] = pack[w]

    def a2a_wait(k, carry):
        peer = (w + k) % wide
        a2a_copy(peer, peer).wait()
        return carry

    lax.fori_loop(1, wide, a2a_wait, 0)

    lane2 = lax.broadcasted_iota(jnp.int32, (HALVES * SUB, LANES), 1)

    for v in range(wide):
        tile = arrived[v]
        x = jnp.concatenate([tile, pltpu.roll(tile, LANES - share, 1)], axis=0)
        x = jnp.where(lane2 < share, x, 0.0)
        high, low = split_pair(x)
        rows = slice(v * HALVES * SUB, (v + 1) * HALVES * SUB)
        fmat[rows, :] = x
        amat[rows, 0:LANES] = (high + pltpu.roll(low, share, 1)).astype(BF16)
        amat[rows, LANES : 2 * LANES] = high.astype(BF16)
        bmat[rows, 0:LANES] = (high + pltpu.roll(high, share, 1)).astype(BF16)
        bmat[rows, LANES : 2 * LANES] = low.astype(BF16)

    tiles = gram.shape[2] // SUB
    chip_here = q // 2

    def place_of(tile):
        chunk, t = divmod(tile, tiles)
        return chunk // 2, chunk % 2, slice(t * SUB, (t + 1) * SUB)

    side = fmat.shape[0] // LANES
    blocks_of = upper_blocks(side)
    for index, (i, j) in enumerate(blocks_of):
        block = lax.dot_general(
            amat[i * LANES : (i + 1) * LANES, :],
            bmat[j * LANES : (j + 1) * LANES, :],
            (((1,), (1,)), ((), ())),
            preferred_element_type=F32,
        )
        for part in range(LANES // SUB):
            chip, side_core, rows = place_of(index * (LANES // SUB) + part)
            gram[chip, side_core, rows, :] = block[part * SUB : (part + 1) * SUB, :]

    half = z_size // 2
    assert tiles <= half == 8
    near = half // 2

    def rows_of(t):
        return pl.ds(pl.multiple_of(t * SUB, SUB), SUB)

    partner = (n + 1 - 2 * core, w)
    same_core = [(peer // 2, device) for peer, device in core_peers]

    def core_copy(t):
        return pltpu.make_async_remote_copy(
            src_ref=gram.at[:, 1 - core, rows_of(t), :],
            dst_ref=core_in.at[t],
            send_sem=core_sent.at[t],
            recv_sem=core_recv.at[t],
            device_id=partner,
            device_id_type=MESH,
        )

    def hand_copy(t):
        return pltpu.make_async_remote_copy(
            src_ref=full.at[:, core, rows_of(t), :],
            dst_ref=full.at[:, core, rows_of(t), :],
            send_sem=hand_sent.at[t],
            recv_sem=hand_recv.at[t],
            device_id=partner,
            device_id_type=MESH,
        )

    def owner_of(i):
        up = jnp.where(i % 2 == 0, (z_size - (i + 1) // 2) % half, (i + 1) // 2)
        up = jnp.where(i == half - 1, near, up)
        t = (3 * ((z + up) % half)) % half
        return up, t < tiles, jnp.minimum(t, tiles - 1)

    def all_bytes(ref, sem):
        pltpu.make_async_copy(ref, ref, sem).wait()

    def core_send(i, carry):
        _, owned, t = owner_of(i)

        @pl.when(owned)
        def _():
            core_copy(t).start()

        return carry

    lax.fori_loop(0, half, core_send, 0)

    def plane_send(i, carry):
        _, owned, t = owner_of(i)

        @pl.when(owned)
        def _():
            core_copy(t).wait_recv()
            core_sum[t] = gram[:, core, rows_of(t), :] + core_in[t]
            for k, (chip, device) in enumerate(same_core):
                pltpu.make_async_remote_copy(
                    src_ref=core_sum.at[t, chip],
                    dst_ref=plane_in.at[t, k],
                    send_sem=plane_sent.at[t],
                    recv_sem=plane_recv.at[t],
                    device_id=device,
                    device_id_type=MESH,
                ).start()

        return carry

    lax.fori_loop(0, half, plane_send, 0)

    def z_copy(up, t, second):
        there = (up + second * half) % z_size
        return pltpu.make_async_remote_copy(
            src_ref=plane_sum.at[t],
            dst_ref=z_in.at[(there + z_size - 1) % z_size],
            send_sem=z_sent.at[t, second],
            recv_sem=z_recv,
            device_id=(n, y * z_size + (z + there) % z_size),
            device_id_type=MESH,
        )

    def bcast_copy(down, t):
        return pltpu.make_async_remote_copy(
            src_ref=z_sum,
            dst_ref=full.at[chip_here, core, rows_of(t), :],
            send_sem=bcast_sent,
            recv_sem=bcast_recv.at[t],
            device_id=(n, y * z_size + (z + z_size - down) % z_size),
            device_id_type=MESH,
        )

    def plane_reduce(i, carry):
        up, owned, t = owner_of(i)

        @pl.when(owned)
        def _():
            all_bytes(plane_in.at[t], plane_recv.at[t])
            plane_sum[t] = core_sum[t, chip_here] + jnp.sum(plane_in[t], axis=0)
            z_copy(up, t, 1).start()

        @pl.when(owned & (up != 0))
        def _():
            z_copy(up, t, 0).start()

        return carry

    lax.fori_loop(0, half, plane_reduce, 0)

    _, owner_here, mine = owner_of(0)

    @pl.when(owner_here)
    def _():
        all_bytes(z_in, z_recv)
        z_sum[...] = plane_sum[mine] + jnp.sum(z_in[...], axis=0)
        for down in [near] + [d for k in range(near - 1, 0, -1) for d in (k, -k)]:
            bcast_copy(down, mine).start()
        full[chip_here, core, rows_of(mine), :] = z_sum[...]

    def gather_send(i, carry):
        up, owned, t = owner_of(i)

        @pl.when(owned & (up != 0))
        def _():
            bcast_copy(near, t).wait_recv()

        @pl.when(owned)
        def _():
            for _, device in same_core:
                pltpu.make_async_remote_copy(
                    src_ref=full.at[chip_here, core, rows_of(t), :],
                    dst_ref=full.at[chip_here, core, rows_of(t), :],
                    send_sem=gather_sent.at[t],
                    recv_sem=gather_recv.at[t],
                    device_id=device,
                    device_id_type=MESH,
                ).start()

        return carry

    lax.fori_loop(0, half, gather_send, 0)

    def hand_over(i, carry):
        _, owned, t = owner_of(i)

        @pl.when(owned)
        def _():
            all_bytes(plane_in.at[t], gather_recv.at[t])
            hand_copy(t).start()

        return carry

    lax.fori_loop(0, half, hand_over, 0)

    for t in range(tiles):
        all_bytes(core_in.at[t], hand_recv.at[t])

    squares = jnp.zeros((SUB, LANES), F32)
    for index, (i, j) in enumerate(blocks_of):
        places = [place_of(index * (LANES // SUB) + part) for part in range(LANES // SUB)]
        block = jnp.concatenate([full[chip, side_core, rows, :] for chip, side_core, rows in places], axis=0)
        power = jnp.sum((block * block).reshape(LANES // SUB, SUB, LANES), axis=0)
        squares = squares + (power if i == j else 2.0 * power)
        high, low = split_pair(block)
        ghi[i * LANES : (i + 1) * LANES, j * LANES : (j + 1) * LANES] = high.astype(BF16)
        glo[i * LANES : (i + 1) * LANES, j * LANES : (j + 1) * LANES] = low.astype(BF16)
        if i != j:
            ghi[j * LANES : (j + 1) * LANES, i * LANES : (i + 1) * LANES] = high.T.astype(BF16)
            glo[j * LANES : (j + 1) * LANES, i * LANES : (i + 1) * LANES] = low.T.astype(BF16)

    frob = jnp.sqrt(jnp.sum(squares, keepdims=True) + 1e-06)
    scale = jnp.sqrt((total * LANES) / frob)
    main = 1.5 * scale
    cross = 0.5 * scale / frob
    fpair = amat[:, 0:LANES]
    for i in range(side):
        rows = slice(i * LANES, (i + 1) * LANES)
        zhi = jnp.dot(ghi[rows, :], fpair, preferred_element_type=F32)
        zlo = jnp.dot(glo[rows, :], fpair, preferred_element_type=F32)
        prod = (pltpu.roll(zhi, LANES - share, 1) + zlo) + zhi
        res = main * fmat[rows, :] - cross * prod
        out_ref[:, rows] = res.T[:share, :]

    for t in range(tiles):
        all_bytes(plane_in.at[t], plane_sent.at[t])
        all_bytes(plane_in.at[t], gather_sent.at[t])
        core_copy(t).wait_send()
        hand_copy(t).wait_send()

    def z_drain(i, carry):
        up, owned, t = owner_of(i)

        @pl.when(owned)
        def _():
            z_copy(up, t, 1).wait_send()

        @pl.when(owned & (up != 0))
        def _():
            z_copy(up, t, 0).wait_send()

        return carry

    lax.fori_loop(0, half, z_drain, 0)

    @pl.when(owner_here)
    def _():
        all_bytes(z_in.at[pl.ds(0, half - 1)], bcast_sent)


def on_device(cfg, vectors, blocks, columns, lower_bound, upper_bound):
    narrow, wide, z_size = cfg
    vecs, width = vectors.shape
    rows_here, slots = columns.shape
    count = vecs * wide
    side = count // LANES
    plane = narrow * (wide // z_size)
    gram_rows = len(upper_blocks(side)) * LANES
    tiles = gram_rows // plane // SUB
    ext = rows_here + 2 * REACH
    smem = pl.BlockSpec(memory_space=pltpu.SMEM)
    vmem = pl.BlockSpec(memory_space=pltpu.VMEM)
    hbm = pl.BlockSpec(memory_space=pltpu.HBM)
    dma = pltpu.SemaphoreType.DMA
    turned = pl.pallas_call(
        functools.partial(kernel_body, cfg),
        out_shape=jax.ShapeDtypeStruct((width // wide, count), F32),
        in_specs=[hbm, smem, smem, hbm, hbm],
        out_specs=vmem,
        scratch_shapes=[
            pltpu.VMEM((STEPS + 1, ext, vecs, LANES), F32),
            pltpu.VMEM((rows_here, 2 * LANES, slots * LANES), BF16),
            pltpu.VMEM((ext + 1, 2 * vecs, LANES), BF16),
            pltpu.VMEM((2, REACH, 2 * LANES, REACH * LANES), BF16),
            pltpu.VMEM((2, REACH, vecs, LANES), F32),
            pltpu.SMEM((rows_here, slots), jnp.int32),
            pltpu.SMEM((rows_here, slots), jnp.int32),
            pltpu.SMEM((slots, rows_here), jnp.int32),
            pltpu.VMEM((rows_here, slots, LANES, LANES), F32),
            pltpu.VMEM((wide, SUB, LANES), F32),
            pltpu.VMEM((wide, SUB, LANES), F32),
            pltpu.VMEM((count, LANES), F32),
            pltpu.VMEM((count, 2 * LANES), BF16),
            pltpu.VMEM((count, 2 * LANES), BF16),
            pltpu.VMEM((plane // 2, 2, tiles * SUB, LANES), F32),
            pltpu.VMEM((tiles, plane // 2, SUB, LANES), F32),
            pltpu.VMEM((tiles, plane // 2, SUB, LANES), F32),
            pltpu.VMEM((tiles, plane // 2 - 1, SUB, LANES), F32),
            pltpu.VMEM((tiles, SUB, LANES), F32),
            pltpu.VMEM((z_size - 1, SUB, LANES), F32),
            pltpu.VMEM((SUB, LANES), F32),
            pltpu.VMEM((plane // 2, 2, tiles * SUB, LANES), F32),
            pltpu.VMEM((count, count), BF16),
            pltpu.VMEM((count, count), BF16),
            dma((2,)),
            dma((rows_here,)),
            pltpu.SemaphoreType.REGULAR((STEPS,)),
            dma((STEPS, 2)),
            dma((STEPS, 2)),
            dma((wide,)),
            dma((wide,)),
            dma((tiles,)),
            dma((tiles,)),
            dma((tiles,)),
            dma((tiles,)),
            dma((tiles,)),
            dma((tiles,)),
            dma((tiles, 2)),
            dma,
            dma,
            dma((tiles,)),
            dma((tiles,)),
            dma((tiles,)),
        ],
        compiler_params=pltpu.CompilerParams(
            collective_id=0, has_side_effects=True, vmem_limit_bytes=67_043_328
        ),
    )(columns.T, lower_bound, upper_bound, vectors, blocks)
    return turned.T


def solution(mesh):
    cfg = (mesh.shape["narrow"], mesh.shape["wide"], Z_SIZE)
    return jax.shard_map(
        functools.partial(on_device, cfg),
        mesh=mesh,
        in_specs=(P("wide", "narrow"), P("narrow", None, None, None), P("narrow", None), P(), P()),
        out_specs=P(None, ("narrow", "wide")),
        check_vma=False,
    )
```
